32 devices in a mesh: dp: 8 (over z, core), fsdp: 4 (over y, x).
Axes of the slice: x: 2, y: 2, z: 4, core: 2. Of those that a mesh axis runs over, the one named last changes fastest.
Arguments:
- hidden_in: bfloat16 [16384, 1024], P(('dp', 'fsdp')), may hold values from -6 to 6
- w_query: bfloat16 [2, 1024, 1024], P(None, ('dp', 'fsdp')), may hold values from -0.1875 to 0.1875
- w_key: bfloat16 [2, 1024, 1024], P(None, ('dp', 'fsdp')), may hold values from -0.1875 to 0.1875
- w_value: bfloat16 [2, 1024, 1024], P(None, ('dp', 'fsdp')), may hold values from -0.1875 to 0.1875
- w_output: bfloat16 [2, 1024, 1024], P(None, ('dp', 'fsdp')), may hold values from -0.1875 to 0.1875
- w_up: bfloat16 [2, 1024, 4096], P(None, ('dp', 'fsdp')), may hold values from -0.1875 to 0.1875
- w_down: bfloat16 [2, 4096, 1024], P(None, ('dp', 'fsdp')), may hold values from -0.09375 to 0.09375
- norm_gain: bfloat16 [2, 4, 1024], P(None, None, ('dp', 'fsdp')), may hold values from 0.25 to 1.75
- norm_bias: bfloat16 [2, 4, 1024], P(None, None, ('dp', 'fsdp')), may hold values from -1.5 to 1.5
- grad_out: bfloat16 [16384, 1024], P(('dp', 'fsdp')), may hold values from -6 to 6
- group_id: int32 [8], replicated, may hold values from 0 to 3
- group_scale: float32 [4], replicated, may hold values from 0.5 to 2
- span_place: int32 [32], replicated, may hold values from 0 to 3, as said below
Outputs:
- hidden_mid: bfloat16 [16384, 1024], P(('dp', 'fsdp'))
- hidden_out: bfloat16 [16384, 1024], P(('dp', 'fsdp'))
- grad_in: float32 [16384, 1024], P(('dp', 'fsdp'))
- grad_query: float32 [2, 1024, 1024], P(None, ('dp', 'fsdp'))
- grad_key: float32 [2, 1024, 1024], P(None, ('dp', 'fsdp'))
- grad_value: float32 [2, 1024, 1024], P(None, ('dp', 'fsdp'))
- grad_projection: float32 [2, 1024, 1024], P(None, ('dp', 'fsdp'))
- grad_up: float32 [2, 1024, 4096], P(None, ('dp', 'fsdp'))
- grad_down: float32 [2, 4096, 1024], P(None, ('dp', 'fsdp'))
- grad_gain: float32 [2, 4, 1024], P(None, None, ('dp', 'fsdp'))
- grad_bias: float32 [2, 4, 1024], P(None, None, ('dp', 'fsdp'))
The draws below stay inside these ranges and needn't reach their ends.
Inputs may be any that keep to these rules, and one draw needn't show every extreme that they name: `span_place`: each aligned group of 4 entries (the spans of one row) is a permutation of 0 to 3.
All inputs are finite; a program needn't handle non-finite values.
Results may differ from the reference program's by a relative error of at most 0.017.
Values may be sent and summed in bfloat16 or wider, within the bound.
No kernel may reach another device: no remote copies, remote signals or barrier semaphores. Data moves between devices by JAX's collectives and lax.ppermute only.
A program may use at most 256 MiB of HBM per device.

```python
import math
import jax
import jax.numpy as jnp
from jax import lax

D = 1024
FF = 4096
HEADS = 16
HEAD_DIM = 64
LAYERS = 2
LEN = 2048
GROUPS = 4
TOK_DEV = 512
SPANS = 4
TOKENS = 16384
ROWS = 8


def draw_span_place(key, part):
    scores = jax.random.randint(key, (ROWS, SPANS), 0, 1 << 20) * SPANS + jnp.arange(SPANS, dtype=jnp.int32)[None, :]
    order = jnp.argsort(scores, axis=1)
    return order.reshape(-1).astype(jnp.int32)


def place_ends(drawn, own_key, least, top_value):
    longest = drawn.shape.index(max(drawn.shape))
    spots = []
    for shift in (0, 1):
        where = [jax.random.randint(jax.random.fold_in(own_key, axis), (), 0, length) for axis, length in enumerate(drawn.shape)]
        where[longest] = (where[longest] + shift) % drawn.shape[longest]
        spots.append(tuple(where))
    return drawn.at[spots[0]].set(least).at[spots[1]].set(top_value)


def levels(stream_key, extent, split, low, top_value):
    level = 1.0
    for axis_at, blocks in split:
        heights = jax.random.uniform(jax.random.fold_in(jax.random.fold_in(stream_key, 6), axis_at), (blocks,), jnp.float32, low / len(split), top_value / len(split))
        level = level * jnp.repeat(jnp.exp(heights), extent[axis_at] // blocks).reshape((-1,) + (1,) * (len(extent) - 1 - axis_at))
    return level


def scatter_about(rng, dims, deviation, bound, cuts=(), kind=jnp.bfloat16):
    entries = jax.random.normal(rng, dims, jnp.float32) * deviation
    if len(cuts) > 0:
        entries = levels(rng, dims, cuts, -0.22, 0.18) * entries
    return jnp.clip(entries, min=-bound, max=bound).astype(kind)


def setup_inputs(seed: int = 0) -> dict:
    splits = jax.random.split(jax.random.key(seed), 14)
    hidden_in = scatter_about(splits[0], (TOKENS, D), 1.0, 6.0, ((0, 32),))
    w_query = scatter_about(splits[1], (LAYERS, D, D), D ** -0.5, 0.1875, ((1, 32),))
    w_key = scatter_about(splits[2], (LAYERS, D, D), D ** -0.5, 0.1875, ((1, 32),))
    w_value = scatter_about(splits[3], (LAYERS, D, D), D ** -0.5, 0.1875, ((1, 32),))
    w_output = scatter_about(splits[4], (LAYERS, D, D), D ** -0.5, 0.1875, ((1, 32),))
    w_up = scatter_about(splits[5], (LAYERS, D, FF), D ** -0.5, 0.1875, ((1, 32),))
    w_down = scatter_about(splits[6], (LAYERS, FF, D), FF ** -0.5, 0.09375, ((1, 32),))
    norm_gain = jnp.clip(1.0 + 0.15 * jax.random.normal(splits[7], (LAYERS, 4, D), jnp.float32), 0.25, 1.75).astype(jnp.bfloat16)
    norm_bias = scatter_about(splits[8], (LAYERS, 4, D), 0.3, 1.5, ((2, 32),))
    grad_out = scatter_about(splits[9], (TOKENS, D), 1.0, 6.0, ((0, 32),))
    group_id = place_ends(jax.random.randint(splits[10], (ROWS,), 0, GROUPS), jax.random.fold_in(splits[10], 1), 0, GROUPS - 1).astype(jnp.int32)
    group_scale = jnp.clip(jnp.exp(jax.random.uniform(splits[11], (GROUPS,), jnp.float32, math.log(0.5), math.log(2.0))), 0.5, 2.0)
    span_place = draw_span_place(jax.random.fold_in(splits[13], 71), 0)
    return dict(hidden_in=hidden_in, w_query=w_query, w_key=w_key, w_value=w_value, w_output=w_output, w_up=w_up, w_down=w_down, norm_gain=norm_gain, norm_bias=norm_bias, grad_out=grad_out, group_id=group_id, group_scale=group_scale, span_place=span_place)


@jax.custom_vjp
def low(v):
    return lax.optimization_barrier(v.astype(jnp.bfloat16)).astype(jnp.float32)

@jax.custom_vjp
def low_back(v):
    return v

def low_keep(v):
    return (low(v), None)

def low_pass(kept, grad):
    return (grad,)

def back_keep(v):
    return (v, None)

def back_low(kept, grad):
    return (low(grad),)
low.defvjp(low_keep, low_pass)
low_back.defvjp(back_keep, back_low)

def matmul(left, right):
    return jnp.dot(left, right, precision=lax.Precision.HIGHEST)

def layer_norm(values, gain_row, bias_row):
    centred = values - lax.optimization_barrier(jnp.mean(values, axis=-1, keepdims=True))
    variance = lax.optimization_barrier(jnp.mean(centred * centred, axis=-1, keepdims=True))
    return centred * lax.rsqrt(variance + 1e-05) * gain_row + bias_row

def rotary(values, positions):
    row_count = values.shape[0]
    head_count = values.shape[1] // HEAD_DIM
    half_dim = HEAD_DIM // 2
    shaped = values.reshape(row_count, head_count, HEAD_DIM)
    frequency = jnp.exp(jnp.arange(half_dim, dtype=jnp.float32) * (-math.log(10000.0) / half_dim))
    angles = positions.astype(jnp.float32)[:, None] * frequency[None, :]
    cosine = jnp.cos(angles)[:, None, :]
    sine_part = jnp.sin(angles)[:, None, :]
    leading = shaped[:, :, :half_dim]
    trailing = shaped[:, :, half_dim:]
    turned = jnp.concatenate([leading * cosine - trailing * sine_part, trailing * cosine + leading * sine_part], axis=-1)
    return turned.reshape(row_count, head_count * HEAD_DIM)

def one_layer(weights, hidden, positions):
    query_weight, key_weight, value_weight, output_weight, up_weight, down_weight, gains, biases = weights
    row_count = hidden.shape[0]
    normed = low(layer_norm(hidden, gains[0], biases[0]))
    queries = low(rotary(low_back(matmul(normed, query_weight)), positions))
    keys = low(rotary(low_back(matmul(normed, key_weight)), positions))
    values = low(low_back(matmul(normed, value_weight)))
    query_heads = queries.reshape(row_count, HEADS, HEAD_DIM)
    key_heads = keys.reshape(row_count, HEADS, HEAD_DIM)
    value_heads = values.reshape(row_count, HEADS, HEAD_DIM)
    scores = jnp.einsum('qhd,khd->hqk', query_heads, key_heads, precision=lax.Precision.HIGHEST) * 0.125
    allowed = positions[None, :] <= positions[:, None]
    scores = low_back(jnp.where(allowed[None, :, :], scores, -1e+30))
    weights_soft = jax.nn.softmax(scores, axis=-1)
    attended = jnp.einsum('hqk,khd->qhd', low(weights_soft), value_heads, precision=lax.Precision.HIGHEST)
    attended = low(low_back(attended.reshape(row_count, HEADS * HEAD_DIM)))
    projected = low_back(matmul(attended, output_weight))
    middle = hidden + layer_norm(projected, gains[1], biases[1])
    mlp_in = low(layer_norm(middle, gains[2], biases[2]))
    up_pre = low_back(matmul(mlp_in, up_weight))
    activated = low(jax.nn.gelu(up_pre))
    down_out = low_back(matmul(activated, down_weight))
    return middle + layer_norm(down_out, gains[3], biases[3])

def row_forward(params, row_hidden, row_positions):
    first = tuple((item[0] for item in params))
    second = tuple((item[1] for item in params))
    middle = low(one_layer(first, row_hidden, row_positions))
    return (middle, one_layer(second, middle, row_positions))

def reference(hidden_in, w_query, w_key, w_value, w_output, w_up, w_down, norm_gain, norm_bias, grad_out, group_id, group_scale, span_place):
    params = tuple((item.astype(jnp.float32) for item in (w_query, w_key, w_value, w_output, w_up, w_down, norm_gain, norm_bias)))
    row_count = hidden_in.shape[0] // LEN
    rows_in = hidden_in.astype(jnp.float32).reshape(row_count, LEN, D)
    places = span_place.reshape(row_count, SPANS)
    positions = (places[:, :, None] * TOK_DEV + jnp.arange(TOK_DEV, dtype=jnp.int32)[None, None, :]).reshape(row_count, LEN).astype(jnp.int32)

    def whole(params_in, hidden_rows):

        def row_step(carry, operands):
            row_hidden, row_positions = operands
            middle, final = row_forward(params_in, row_hidden, row_positions)
            return (carry, (middle, final))
        _, (middles, finals) = lax.scan(jax.checkpoint(row_step), 0, (hidden_rows, positions))
        return (finals, middles)
    finals, backward, middles = jax.vjp(whole, params, rows_in, has_aux=True)
    row_scales = group_scale.astype(jnp.float32)[group_id]
    cotangent = grad_out.astype(jnp.float32).reshape(row_count, LEN, D) * row_scales[:, None, None]
    grad_params, grad_rows = backward(cotangent)
    return (middles.reshape(row_count * LEN, D).astype(jnp.bfloat16), finals.reshape(row_count * LEN, D).astype(jnp.bfloat16), grad_rows.reshape(row_count * LEN, D), grad_params[0], grad_params[1], grad_params[2], grad_params[3], grad_params[4], grad_params[5], grad_params[6], grad_params[7])
```

```python
import functools
import math

import jax
import jax.numpy as jnp
from jax import lax
from jax.experimental import pallas as pl
from jax.experimental.pallas import tpu as pltpu
from jax.sharding import Mesh
from jax.sharding import PartitionSpec as P

HEAD_DIM = 64
TOK_DEV = 512
VMEM = 60 << 20
SPANS = 4


masked_score = -1e30
score_factor = 0.125


def product_rows(left, right):
    return lax.dot_general(
        left, right, (((0,), (0,)), ((), ())), preferred_element_type=jnp.float32
    )


NT = (((1,), (1,)), ((), ()))
NN = (((1,), (0,)), ((), ()))
TN = (((0,), (0,)), ((), ()))
PAIR = 2 * HEAD_DIM
PAIRS = 2


def mul(left, right, how):
    return lax.dot_general(left, right, how, preferred_element_type=jnp.float32)


def lane_in_head(parity, shape):
    lanes = lax.broadcasted_iota(jnp.int32, shape, 1)
    return (lanes // HEAD_DIM) == parity


def short():
    return pl.CostEstimate(flops=1000, bytes_accessed=1000, transcendentals=0)


def whole_vmem():
    return pl.BlockSpec(memory_space=pltpu.VMEM)


def attend_kernel(places, pieces, outs, lse_ref, row, keys, values, scores, turned):
    head, block = pl.program_id(0), pl.program_id(1)
    span, width = outs.shape[1:]

    @pl.when((head == 0) & (block == 0))
    def _():
        for at in range(SPANS):
            row[places[at]] = pieces[at, :, :width] * score_factor
            keys[places[at]] = pieces[at, :, width : 2 * width]
            values[places[at]] = pieces[at, :, 2 * width :]

    parity = head % 2
    lanes = pl.ds(pl.multiple_of((head // 2) * PAIR, PAIR), PAIR)
    inside = lane_in_head(parity, (span, PAIR))
    queries = row[block, :, lanes]
    queries = jnp.where(inside, queries, jnp.zeros_like(queries))

    def first(at, highest):
        tile = mul(queries, keys[at, :, lanes], NT)
        scores[at] = tile
        for part in range(span // 128):
            highest = jnp.maximum(highest, tile[:, part * 128 : (part + 1) * 128])
        return highest

    highest = lax.fori_loop(0, block, first, jnp.full((span, 128), masked_score, jnp.float32))
    tile = mul(queries, keys[block, :, lanes], NT)
    later = lax.broadcasted_iota(jnp.int32, tile.shape, 1) > lax.broadcasted_iota(jnp.int32, tile.shape, 0)
    tile = jnp.where(later, masked_score, tile)
    scores[block] = tile
    for part in range(span // 128):
        highest = jnp.maximum(highest, tile[:, part * 128 : (part + 1) * 128])
    highest = jnp.max(highest, axis=1, keepdims=True)

    def second(at, total):
        weights = jnp.exp(scores[at] - highest).astype(jnp.bfloat16)
        extended = values[at, :, lanes]
        extended = jnp.where(inside, extended, jnp.ones_like(extended))
        return total + mul(weights, extended, NN)

    total = lax.fori_loop(0, block + 1, second, jnp.zeros((span, PAIR), jnp.float32))
    swapped = pltpu.roll(total, HEAD_DIM, 1)
    sums = jnp.where(inside, swapped, total)
    lse_ref[0, 0] = highest + jnp.log(sums)
    mine = (total / sums).astype(jnp.bfloat16)
    turned[block, :, lanes] = jnp.where(inside, mine, turned[block, :, lanes])

    @pl.when((head == pl.num_programs(0) - 1) & (block == SPANS - 1))
    def _():
        for at in range(SPANS):
            outs[at] = turned[places[at]]


def attend(places, pieces):
    _, span, triple = pieces.shape
    width = triple // 3
    heads = width // HEAD_DIM
    flops = heads * 20 * 2 * 2 * span * span * HEAD_DIM // 2
    return pl.pallas_call(
        attend_kernel,
        grid_spec=pltpu.PrefetchScalarGridSpec(
            num_scalar_prefetch=1,
            grid=(heads, SPANS),
            in_specs=[whole_vmem()],
            out_specs=[whole_vmem(), pl.BlockSpec((1, 1, span, PAIR), lambda h, b, p: (h, b, 0, 0))],
            scratch_shapes=[pltpu.VMEM((SPANS, span, width), jnp.bfloat16)] * 3
            + [
                pltpu.VMEM((SPANS, span, span), jnp.float32),
                pltpu.VMEM((SPANS, span, width), jnp.bfloat16),
            ],
        ),
        out_shape=[
            jax.ShapeDtypeStruct((SPANS, span, width), jnp.bfloat16),
            jax.ShapeDtypeStruct((heads, SPANS, span, PAIR), jnp.float32),
        ],
        compiler_params=pltpu.CompilerParams(vmem_limit_bytes=VMEM),
        cost_estimate=short(),
        name="attend",
    )(places, pieces)


def other_half(values):
    half = HEAD_DIM // 2
    size = values.shape[1]
    lanes = lax.broadcasted_iota(jnp.int32, values.shape, 1)
    return jnp.where(
        lanes % HEAD_DIM < half, pltpu.roll(values, size - half, 1), pltpu.roll(values, half, 1)
    )


def turn(values, cosine, sine):
    return values * cosine + other_half(values) * sine


def turn_back(values, cosine, sine):
    return values * cosine - other_half(values) * sine


def attend_back_kernel(places, pieces, grads, attended, cosine_ref, sine_ref, lse_ref, outs, *held):
    row, keys, values, back, ahead, grad_q, grad_k, grad_v = held
    head, block = pl.program_id(0), pl.program_id(1)
    span, width = grads.shape[1:]

    @pl.when((head == 0) & (block == 0))
    def _():
        for at in range(SPANS):
            row[places[at]] = pieces[at, :, :width] * score_factor
            keys[places[at]] = pieces[at, :, width : 2 * width]
            values[places[at]] = pieces[at, :, 2 * width :]
            back[places[at]] = grads[at]
            ahead[places[at]] = attended[at]
        grad_q[...] = jnp.zeros_like(grad_q)
        grad_k[...] = jnp.zeros_like(grad_k)
        grad_v[...] = jnp.zeros_like(grad_v)

    parity = head % 2
    lanes = pl.ds(pl.multiple_of((head // 2) * PAIR, PAIR), PAIR)
    inside = lane_in_head(parity, (span, PAIR))
    only = lambda value: jnp.where(inside, value, jnp.zeros_like(value))
    queries = only(row[block, :, lanes])
    grad_out = only(back[block, :, lanes])
    lse_row = jnp.transpose(lse_ref[0, 0])[:1]
    terms = grad_out.astype(jnp.float32) * ahead[block, :, lanes].astype(jnp.float32)
    terms_row = jnp.sum(jnp.transpose(terms), axis=0, keepdims=True)

    def tile(at, masked):
        key_tile = keys[at, :, lanes]
        scores = mul(key_tile, queries, NT) - lse_row
        if masked:
            later = lax.broadcasted_iota(jnp.int32, scores.shape, 0) > lax.broadcasted_iota(
                jnp.int32, scores.shape, 1
            )
            scores = jnp.where(later, masked_score, scores)
        weights = jnp.exp(scores)
        grad_weights = mul(values[at, :, lanes], grad_out, NT)
        grad_scores = (weights * (grad_weights - terms_row)).astype(jnp.bfloat16)
        grad_v[at, :, lanes] += mul(weights.astype(jnp.bfloat16), grad_out, NN)
        grad_k[at, :, lanes] += mul(grad_scores, queries, NN)
        return mul(grad_scores, only(key_tile), TN)

    total = lax.fori_loop(
        0, block, lambda at, total: total + tile(at, False), jnp.zeros((span, PAIR), jnp.float32)
    )
    grad_q[block, :, lanes] += total + tile(block, True)

    @pl.when((head == pl.num_programs(0) - 1) & (block == SPANS - 1))
    def _():
        for at in range(SPANS):
            place = places[at]
            cosine, sine = cosine_ref[place], sine_ref[place]
            for pair in range(width // PAIR):
                part = slice(pair * PAIR, (pair + 1) * PAIR)
                outs[at, :, pair * PAIR : (pair + 1) * PAIR] = turn_back(
                    grad_q[place, :, part] * score_factor, cosine, sine
                ).astype(jnp.bfloat16)
                outs[at, :, width + pair * PAIR : width + (pair + 1) * PAIR] = turn_back(
                    grad_k[place, :, part], cosine, sine
                ).astype(jnp.bfloat16)
            outs[at, :, 2 * width :] = grad_v[place].astype(jnp.bfloat16)


def attend_back(places, pieces, grads, attended, cosine, sine, lse):
    _, span, width = grads.shape
    heads = width // HEAD_DIM
    flops = heads * 20 * 2 * 5 * span * span * HEAD_DIM // 2
    stored = lambda kind: pltpu.VMEM((SPANS, span, width), kind)
    return pl.pallas_call(
        attend_back_kernel,
        grid_spec=pltpu.PrefetchScalarGridSpec(
            num_scalar_prefetch=1,
            grid=(heads, SPANS),
            in_specs=[whole_vmem()] * 5
            + [pl.BlockSpec((1, 1, span, PAIR), lambda h, b, p: (h, b, 0, 0))],
            out_specs=whole_vmem(),
            scratch_shapes=[stored(jnp.bfloat16)] * 5 + [stored(jnp.float32)] * 3,
        ),
        out_shape=jax.ShapeDtypeStruct((SPANS, span, 3 * width), jnp.bfloat16),
        compiler_params=pltpu.CompilerParams(vmem_limit_bytes=VMEM),
        cost_estimate=short(),
        name="attend_back",
    )(places, pieces, grads, attended, cosine, sine, lse)


def turning_tables(count):
    half = HEAD_DIM // 2
    frequency = jnp.exp(jnp.arange(half, dtype=jnp.float32) * (-math.log(10000.0) / half))
    angles = jnp.arange(count, dtype=jnp.float32)[:, None] * frequency[None, :]
    cosine, sine = jnp.cos(angles), jnp.sin(angles)
    cosine = jnp.concatenate([cosine] * 4, axis=1)
    sine = jnp.concatenate([-sine, sine, -sine, sine], axis=1)
    shape = (count // TOK_DEV, TOK_DEV, PAIR)
    return (cosine.reshape(shape), sine.reshape(shape))


ROWS = 64
norm_epsilon = 1e-05


def row_loop(count, body, carry):
    size = min(ROWS, count)
    return lax.fori_loop(
        0, count // size, lambda i, c: body(pl.ds(pl.multiple_of(i * size, size), size), c), carry
    )


def normal(values):
    centred = values - jnp.mean(values, axis=-1, keepdims=True)
    inverse = lax.rsqrt(jnp.mean(centred * centred, axis=-1, keepdims=True) + norm_epsilon)
    return (centred * inverse, inverse)


def norm_back(values, grad, gain):
    shape, inverse = normal(values)
    inner = grad * gain
    result = inverse * (
        inner
        - jnp.mean(inner, axis=-1, keepdims=True)
        - shape * jnp.mean(inner * shape, axis=-1, keepdims=True)
    )
    return (
        result,
        jnp.sum(grad * shape, axis=0, keepdims=True),
        jnp.sum(grad, axis=0, keepdims=True),
    )


def fixed(shape):
    return pl.BlockSpec(shape, lambda i: (0,) * len(shape), pipeline_mode=pl.Buffered(1))


def output_spec(block, model):
    return pl.BlockSpec((model, model), lambda i: (0, block), pipeline_mode=pl.Buffered(1))


def project_in_kernel(x_ref, vec_ref, cos_ref, sin_ref, wq_ref, wk_ref, wv_ref, normed_ref, *outs):
    tokens = x_ref.shape[0]

    @pl.when(pl.program_id(0) == 0)
    def _():
        def body(rows, carry):
            shape, _ = normal(x_ref[rows, :].astype(jnp.float32))
            normed_ref[rows, :] = (shape * vec_ref[0:1, :] + vec_ref[4:5, :]).astype(jnp.bfloat16)
            return carry

        row_loop(tokens, body, 0)

    for at, weight_ref in enumerate((wq_ref, wk_ref, wv_ref)):
        made = mul(normed_ref[...], weight_ref[...], NN)
        for pair, out in enumerate(outs):
            part = made[:, pair * PAIR : (pair + 1) * PAIR]
            if at < 2:
                part = turn(part, cos_ref[...], sin_ref[...])
            out[0, :, at * PAIR : (at + 1) * PAIR] = part.astype(jnp.bfloat16)


def weight_spec(weight, first, model):
    return pl.BlockSpec((model, model // SPANS), lambda r: (0, first + r))


def project_in(x, vectors, cosine, sine, weights):
    tokens, model = x.shape
    cost = short()
    piece = pl.BlockSpec((1, tokens, 3 * PAIR), lambda r: (r, 0, 0))
    result = pl.pallas_call(
        project_in_kernel,
        grid=(SPANS,),
        in_specs=[fixed(x.shape), fixed(vectors.shape), fixed(cosine.shape), fixed(sine.shape)]
        + [weight_spec(weight, first, model) for weight, first in weights],
        out_specs=[fixed((tokens, model))] + [piece] * PAIRS,
        out_shape=[jax.ShapeDtypeStruct((tokens, model), jnp.bfloat16)]
        + [jax.ShapeDtypeStruct((SPANS, tokens, 3 * PAIR), jnp.bfloat16)] * PAIRS,
        compiler_params=pltpu.CompilerParams(vmem_limit_bytes=VMEM),
        cost_estimate=cost,
        name="project_in",
    )(x, vectors, cosine, sine, *[weight for weight, _ in weights])
    return (result[0], result[1:])


def project_back_kernel(*refs):
    pieces, refs = refs[:PAIRS], refs[PAIRS:]
    x_ref, vec_ref, gh_ref, wq_ref, wk_ref, wv_ref, gx_ref, sums_ref, joined_ref, total = refs
    step = pl.program_id(0)
    tokens, model = x_ref.shape
    width = wq_ref.shape[1]
    made = None
    for at, weight_ref in enumerate((wq_ref, wk_ref, wv_ref)):
        part = jnp.concatenate(
            [piece[0, :, at * PAIR : (at + 1) * PAIR] for piece in pieces], axis=1
        )
        first = at * model + step * width
        joined_ref[:, pl.ds(pl.multiple_of(first, width), width)] = part
        one = mul(part, weight_ref[...], NT)
        made = one if made is None else made + one

    @pl.when(step == 0)
    def _():
        total[...] = made

    @pl.when(step > 0)
    def _():
        total[...] += made

    @pl.when(step == SPANS - 1)
    def _():
        def body(rows, carry):
            back, gain, bias = norm_back(
                x_ref[rows, :].astype(jnp.float32), total[rows, :], vec_ref[0:1, :]
            )
            gx_ref[rows, :] = gh_ref[rows, :] + back
            return (carry[0] + gain, carry[1] + bias)

        zero = jnp.zeros((1, model), jnp.float32)
        gain, bias = row_loop(tokens, body, (zero, zero))
        sums_ref[...] = jnp.zeros_like(sums_ref)
        sums_ref[0:1, :] = gain
        sums_ref[4:5, :] = bias


def project_back(pieces, x, vectors, grad_middle, weights):
    tokens, model = x.shape
    cost = short()
    return pl.pallas_call(
        project_back_kernel,
        grid=(SPANS,),
        in_specs=[pl.BlockSpec((1, tokens, 3 * PAIR), lambda r: (r, 0, 0))] * PAIRS
        + [fixed(x.shape), fixed(vectors.shape), fixed(x.shape)]
        + [weight_spec(weight, first, model) for weight, first in weights],
        out_specs=[fixed(x.shape), fixed((8, model)), fixed((tokens, 3 * model))],
        scratch_shapes=[pltpu.VMEM((tokens, model), jnp.float32)],
        out_shape=[
            jax.ShapeDtypeStruct((tokens, model), jnp.float32),
            jax.ShapeDtypeStruct((8, model), jnp.float32),
            jax.ShapeDtypeStruct((tokens, 3 * model), jnp.bfloat16),
        ],
        compiler_params=pltpu.CompilerParams(vmem_limit_bytes=VMEM),
        cost_estimate=cost,
        name="project_back",
    )(*pieces, x, vectors, grad_middle, *[weight for weight, _ in weights])


def gelu_parts(z):
    root = math.sqrt(2.0 / math.pi)
    square = z * z
    bent = jnp.tanh(root * z * (1.0 + 0.044715 * square))
    half = 0.5 * (1.0 + bent)
    slope = half + 0.5 * z * (1.0 - bent * bent) * (root * (1.0 + 3.0 * 0.044715 * square))
    return (z * half, slope)


FF_TILE = 512


def feed_kernel(*refs):
    pieces, refs = refs[:PAIRS], refs[PAIRS:]
    x_ref, vec_ref, wo_ref, up_ref, down_ref = refs[:5]
    joined_ref, u_ref, h_ref, c_ref, f_ref, slope_ref, m_ref, y_ref = refs[5:13]
    (held,) = refs[13:]
    step = pl.program_id(0)
    tokens = x_ref.shape[0]

    @pl.when(step == 0)
    def _():
        for pair in range(PAIRS):
            for at in range(SPANS):
                first = (at * PAIRS + pair) * PAIR
                joined_ref[:, first : first + PAIR] = pieces[pair][at]
        u_ref[...] = mul(joined_ref[...], wo_ref[...], NN)

        def body(rows, carry):
            shape, _ = normal(u_ref[rows, :])
            middle = x_ref[rows, :].astype(jnp.float32) + shape * vec_ref[1:2, :] + vec_ref[5:6, :]
            h_ref[rows, :] = middle
            shape, _ = normal(middle)
            c_ref[rows, :] = (shape * vec_ref[2:3, :] + vec_ref[6:7, :]).astype(jnp.bfloat16)
            return carry

        row_loop(tokens, body, 0)

    held[...] = mul(c_ref[...], up_ref[...], NN)

    def bend(rows, carry):
        made, slope = gelu_parts(held[rows, :])
        f_ref[rows, :] = made.astype(jnp.bfloat16)
        slope_ref[rows, :] = slope.astype(jnp.bfloat16)
        return carry

    row_loop(tokens, bend, 0)
    made = mul(f_ref[...], down_ref[...], NN)

    @pl.when(step == 0)
    def _():
        m_ref[...] = made

    @pl.when(step > 0)
    def _():
        m_ref[...] += made

    @pl.when(step == pl.num_programs(0) - 1)
    def _():
        def body(rows, carry):
            shape, _ = normal(m_ref[rows, :])
            result = h_ref[rows, :] + shape * vec_ref[3:4, :] + vec_ref[7:8, :]
            y_ref[rows, :] = result.astype(jnp.bfloat16)
            return carry

        row_loop(tokens, body, 0)


def feed(pieces, x, vectors, output_weight, up_weight, down_weight):
    tokens, model = x.shape
    hidden = up_weight.shape[1]
    full = lambda kind, columns=model: jax.ShapeDtypeStruct((tokens, columns), kind)
    wide = pl.BlockSpec((tokens, FF_TILE), lambda i: (0, i))
    cost = short()
    return pl.pallas_call(
        feed_kernel,
        grid=(hidden // FF_TILE,),
        in_specs=[fixed((SPANS, tokens, PAIR))] * PAIRS
        + [fixed(x.shape), fixed(vectors.shape), output_spec(output_weight[1], model)]
        + [
            pl.BlockSpec((model, FF_TILE), lambda i: (0, i)),
            pl.BlockSpec((FF_TILE, model), lambda i: (i, 0)),
        ],
        out_specs=[fixed(x.shape)] * 4 + [wide, wide] + [fixed(x.shape)] * 2,
        scratch_shapes=[pltpu.VMEM((tokens, FF_TILE), jnp.float32)],
        out_shape=[
            full(jnp.bfloat16),
            full(jnp.float32),
            full(jnp.float32),
            full(jnp.bfloat16),
            full(jnp.bfloat16, hidden),
            full(jnp.bfloat16, hidden),
            full(jnp.float32),
            full(jnp.bfloat16),
        ],
        compiler_params=pltpu.CompilerParams(vmem_limit_bytes=VMEM),
        cost_estimate=cost,
        name="feed",
    )(*pieces, x, vectors, output_weight[0], up_weight, down_weight)


def feed_back_kernel(*refs):
    gy_ref, m_ref, h_ref, u_ref, vec_ref, wo_ref, slope_ref, down_ref, up_ref = refs[:9]
    gm_ref, gz_ref, gh_ref, gu_ref, sums_ref = refs[9:14]
    pieces = refs[14 : 14 + PAIRS]
    total, back = refs[14 + PAIRS :]
    step = pl.program_id(0)
    tokens, model = gy_ref.shape
    zero = jnp.zeros((1, model), jnp.float32)

    @pl.when(step == 0)
    def _():
        def body(rows, carry):
            grad, gain, bias = norm_back(m_ref[rows, :], gy_ref[rows, :], vec_ref[3:4, :])
            gm_ref[rows, :] = grad.astype(jnp.bfloat16)
            return (carry[0] + gain, carry[1] + bias)

        gain, bias = row_loop(tokens, body, (zero, zero))
        sums_ref[0:1, :] = zero
        sums_ref[4:5, :] = zero
        sums_ref[3:4, :] = gain
        sums_ref[7:8, :] = bias

    gz_ref[...] = (mul(gm_ref[...], down_ref[...], NT) * slope_ref[...].astype(jnp.float32)).astype(
        jnp.bfloat16
    )
    made = mul(gz_ref[...], up_ref[...], NT)

    @pl.when(step == 0)
    def _():
        total[...] = made

    @pl.when(step > 0)
    def _():
        total[...] += made

    @pl.when(step == pl.num_programs(0) - 1)
    def _():
        def body(rows, carry):
            grad, gain_two, bias_two = norm_back(h_ref[rows, :], total[rows, :], vec_ref[2:3, :])
            middle = gy_ref[rows, :] + grad
            gh_ref[rows, :] = middle
            grad, gain_one, bias_one = norm_back(u_ref[rows, :], middle, vec_ref[1:2, :])
            gu_ref[rows, :] = grad.astype(jnp.bfloat16)
            new = (gain_one, gain_two, bias_one, bias_two)
            return tuple(old + more for old, more in zip(carry, new))

        gain_one, gain_two, bias_one, bias_two = row_loop(tokens, body, (zero,) * 4)
        sums_ref[1:2, :] = gain_one
        sums_ref[2:3, :] = gain_two
        sums_ref[5:6, :] = bias_one
        sums_ref[6:7, :] = bias_two
        back[...] = mul(gu_ref[...], wo_ref[...], NT).astype(jnp.bfloat16)
        for pair in range(PAIRS):
            for at in range(SPANS):
                first = (at * PAIRS + pair) * PAIR
                pieces[pair][at] = back[:, first : first + PAIR]


def feed_back(grad, m, h, u, vectors, output_weight, slope, down_weight, up_weight):
    tokens, model = grad.shape
    hidden = up_weight.shape[1]
    full = lambda kind, columns=model: jax.ShapeDtypeStruct((tokens, columns), kind)
    wide = pl.BlockSpec((tokens, FF_TILE), lambda i: (0, i))
    cost = short()
    result = pl.pallas_call(
        feed_back_kernel,
        grid=(hidden // FF_TILE,),
        in_specs=[fixed(grad.shape)] * 4
        + [fixed(vectors.shape), output_spec(output_weight[1], model), wide]
        + [
            pl.BlockSpec((FF_TILE, model), lambda i: (i, 0)),
            pl.BlockSpec((model, FF_TILE), lambda i: (0, i)),
        ],
        out_specs=[fixed(grad.shape), wide, fixed(grad.shape), fixed(grad.shape)]
        + [fixed((8, model))]
        + [fixed((SPANS, tokens, PAIR))] * PAIRS,
        scratch_shapes=[
            pltpu.VMEM((tokens, model), jnp.float32),
            pltpu.VMEM((tokens, model), jnp.bfloat16),
        ],
        out_shape=[
            full(jnp.bfloat16),
            full(jnp.bfloat16, hidden),
            full(jnp.float32),
            full(jnp.bfloat16),
            jax.ShapeDtypeStruct((8, model), jnp.float32),
        ]
        + [jax.ShapeDtypeStruct((SPANS, tokens, PAIR), jnp.bfloat16)] * PAIRS,
        compiler_params=pltpu.CompilerParams(vmem_limit_bytes=VMEM),
        cost_estimate=cost,
        name="feed_back",
    )(grad, m, h, u, vectors, output_weight[0], slope, down_weight, up_weight)
    return (result[:5], list(result[5:]))


def weave_kernel(mine, own_ref, other_ref, out_ref):
    count = own_ref.shape[1]
    first = pl.multiple_of(mine[0] * count, count)
    second = pl.multiple_of((1 - mine[0]) * count, count)
    out_ref[0, pl.ds(first, count), :] = own_ref[0]
    out_ref[0, pl.ds(second, count), :] = other_ref[0]


def weave(own, other, mine):
    outer, count, columns = own.shape
    if count % 16 or columns % 128:
        return jnp.where(
            mine == 0, jnp.concatenate([own, other], axis=1), jnp.concatenate([other, own], axis=1)
        )
    spec = pl.BlockSpec((1, count, columns), lambda i, s: (i, 0, 0))
    return pl.pallas_call(
        weave_kernel,
        grid_spec=pltpu.PrefetchScalarGridSpec(
            num_scalar_prefetch=1,
            grid=(outer,),
            in_specs=[spec, spec],
            out_specs=pl.BlockSpec((1, 2 * count, columns), lambda i, s: (i, 0, 0)),
        ),
        out_shape=jax.ShapeDtypeStruct((outer, 2 * count, columns), own.dtype),
        compiler_params=pltpu.CompilerParams(vmem_limit_bytes=VMEM),
        cost_estimate=short(),
        name="weave",
    )(jnp.reshape(mine, (1,)), own, other)


def half_kernel(which, *refs, far, near, start):
    lefts, (right_ref, *more, out_ref, turned) = refs[:far], refs[far:]

    @pl.when(pl.program_id(0) == 0)
    def _():
        for at, left_ref in enumerate(lefts):
            size = left_ref.shape[1]
            turned[at * size : (at + 1) * size, :] = jnp.transpose(left_ref[...])

    made = mul(turned[...], right_ref[...], NN)
    if not more:
        out_ref[...] = made.astype(out_ref.dtype)
        return
    made = (made + more[0][...].astype(jnp.float32)).astype(out_ref.dtype)
    rows = out_ref.shape[2]
    for z in range(far):
        for f in range(near):
            at = (z * near + f) * rows
            out_ref[f, z] = made[at : at + rows]


def half_rows_kernel(which, left_ref, right_ref, *refs, near):
    out_ref = refs[-1]
    made = mul(left_ref[...], right_ref[...], TN)
    if len(refs) == 1:
        out_ref[...] = made.astype(out_ref.dtype)
        return
    made = (made + refs[0][...].astype(jnp.float32)).astype(out_ref.dtype)
    rows, columns = out_ref.shape[2], made.shape[1]
    for f in range(near):
        for q in range(out_ref.shape[3] // columns):
            at = f * (made.shape[0] // near) + q * rows
            out_ref[f, 0, :, q * columns : (q + 1) * columns] = made[at : at + rows]


def half_product(left, right, which, far, near, got=None, joint=None, start=0, width=0, rows=0):
    tokens, count = left.shape
    columns = right.shape[1]
    size = count // (2 * far)
    which = jnp.reshape(which, (1,))
    tall = size // near > rows if got is not None else count > columns
    tile = columns if tall else min(columns, 1024)
    if tall:
        grid = (far,)
        ins = [
            pl.BlockSpec((tokens, size), lambda i, w: (0, 2 * i + w[0])),
            pl.BlockSpec((tokens, columns), lambda i, w: (0, 0)),
        ]
        lefts, scratch = [left], []
        flat = pl.BlockSpec((size, columns), lambda i, w: (i, 0))
        wide = columns * (size // near // rows) if got is not None else 0
        spread = pl.BlockSpec((near, 1, rows, wide), lambda i, w: (0, i, 0, start // wide))
        kernel = functools.partial(half_rows_kernel, near=near)
    else:
        grid = (columns // tile,)
        ins = [
            pl.BlockSpec((tokens, size), lambda c, w, at=at: (0, 2 * at + w[0])) for at in range(far)
        ] + [pl.BlockSpec((tokens, tile), lambda c, w: (0, c))]
        lefts, scratch = [left] * far, [pltpu.VMEM((count // 2, tokens), jnp.bfloat16)]
        flat = pl.BlockSpec((count // 2, tile), lambda c, w: (0, c))
        spread = pl.BlockSpec((near, far, rows, tile), lambda c, w: (0, 0, 0, start // tile + c))
        kernel = functools.partial(half_kernel, far=far, near=near, start=start)
    operands, aliases = ([*lefts, right], {})
    if got is None:
        shape, out = (count // 2, columns), flat
    else:
        shape, out = (near, far, rows, width), spread
        operands.append(got)
        ins.append(flat)
        if joint is not None:
            plain = kernel
            kernel = lambda *refs: plain(*refs[: 1 + len(operands) - 1], *refs[1 + len(operands) :])
            operands.append(joint)
            ins.append(pl.BlockSpec(memory_space=pl.ANY))
            aliases = {len(operands): 0}
    return pl.pallas_call(
        kernel,
        grid_spec=pltpu.PrefetchScalarGridSpec(
            num_scalar_prefetch=1, grid=grid, in_specs=ins, out_specs=out, scratch_shapes=scratch
        ),
        out_shape=jax.ShapeDtypeStruct(shape, jnp.bfloat16),
        input_output_aliases=aliases,
        compiler_params=pltpu.CompilerParams(vmem_limit_bytes=VMEM),
        cost_estimate=short(),
        name="half_product",
    )(which, *operands)


def sizes():
    return (lax.axis_size("far"), lax.axis_size("core"), lax.axis_size("fsdp"))


def flip(array, axis, apart):
    return lax.ppermute(array, axis, [(i, i ^ apart) for i in range(lax.axis_size(axis))])


def swap_cores(array):
    return flip(array, "core", 1)


def after(values, *others):
    return lax.optimization_barrier((values, others))[0]


def exchange(pieces):
    count = lax.axis_size("fsdp")
    rows = [list(range(at, at + SPANS)) for at in range(0, count, SPANS)]
    return lax.all_to_all(
        pieces, "fsdp", 0, 0, axis_index_groups=rows if len(rows) > 1 else None, tiled=True
    )


class Gather:
    def __init__(self, part, inner_first):
        far, _, near = sizes()
        steps = lambda axis, count: [(axis, i) for i in range(count.bit_length() - 1)]
        inner = steps("fsdp", near)
        if inner_first:
            inner = inner[1::-1] + inner[2:]
        self.part = part
        self.order = steps("far", far)[::-1] + inner + [("core", 0)]
        self.place = {bit: at for at, bit in enumerate(steps("fsdp", near) + [("core", 0)] + steps("far", far))}
        self.held = []

    def run(self, count=None):
        for _ in range(len(self.order) if count is None else count):
            bit = self.order.pop(0)
            outer = 2 ** sum(1 for other in self.held if self.place[other] > self.place[bit])
            rows, columns = self.part.shape
            own = self.part.reshape(outer, rows // outer, columns)
            other = flip(own, bit[0], 1 << bit[1])
            mine = lax.axis_index(bit[0]) >> bit[1] & 1
            self.part = weave(own, other, mine).reshape(2 * rows, columns)
            self.held.append(bit)
        return self.part


class Reduction:
    def __init__(self, products):
        self.products = products
        far, core, near = sizes()
        self.rows = products[0][0].shape[1] // (far * core * near)
        self.plain = self.rows % 16 != 0
        self.stage = 0
        self.value = ()
        if not self.plain:
            self.value = [
                half_product(left, right, 1 - lax.axis_index("core"), far, near)
                for left, right in products
            ]

    def swap(self):
        if not self.plain:
            self.got = [swap_cores(value) for value in self.value]
            self.value = ()

    def join(self):
        if self.plain:
            return
        far, core, near = sizes()
        block = self.rows * far * near
        width = sum(value.size for value in self.got) // block
        joint, start = None, 0
        for (left, right), got in zip(self.products, self.got):
            joint = half_product(
                left, right, lax.axis_index("core"), far, near, got, joint, start, width, self.rows
            )
            start += got.size // block
        self.value = joint

    def near(self, offload):
        if self.plain:
            return
        count, far, rows, width = self.value.shape
        flat = self.value.reshape(count * far * rows, width)
        if offload:
            self.value = lax.psum_scatter(flat, "fsdp", scatter_dimension=0, tiled=True)
        else:
            got = lax.all_to_all(flat, "fsdp", 0, 0, tiled=True).reshape(count, far * rows, width)
            self.value = jnp.sum(got.astype(jnp.float32), axis=0).astype(jnp.bfloat16)

    def far(self):
        if self.plain:
            return
        value = self.value.reshape(lax.axis_size("far"), self.rows, self.value.shape[-1])
        apart = 1
        while value.shape[0] > 1:
            mine = lax.axis_index("far") // apart % 2
            split = value.reshape(value.shape[0] // 2, 2, *value.shape[1:])
            pick = lambda at: lax.dynamic_index_in_dim(split, at, 1, keepdims=False)
            got = flip(pick(1 - mine), "far", apart)
            value = pick(mine).astype(jnp.float32) + got.astype(jnp.float32)
            if value.shape[0] > 1:
                value = value.astype(jnp.bfloat16)
            apart *= 2
        self.value = value

    def result(self):
        if self.plain:
            sums = [
                lax.psum_scatter(
                    product_rows(left, right), ("far", "core", "fsdp"), scatter_dimension=0, tiled=True
                )
                for left, right in self.products
            ]
            return sums
        total = jnp.sum(self.value.astype(jnp.float32), axis=0)
        sums, first = ([], 0)
        for left, right in self.products:
            count = left.shape[1] // self.products[0][0].shape[1]
            columns = right.shape[1]
            part = total[:, first : first + count * columns]
            part = part.reshape(self.rows, count, columns).transpose(1, 0, 2)
            sums.append(part.reshape(count * self.rows, columns))
            first += count * columns
        return sums


def tie(main, *reductions):
    main, values = lax.optimization_barrier((main, [reduction.value for reduction in reductions]))
    for reduction, value in zip(reductions, values):
        reduction.value = value
    return main


def sum_vectors(terms):
    far, core, near = sizes()
    for axis, count in (("core", core), ("fsdp", near), ("far", far)):
        for bit in range(count.bit_length() - 1):
            terms = terms + flip(terms, axis, 1 << bit)
    slot = (lax.axis_index("far") * core + lax.axis_index("core")) * near + lax.axis_index("fsdp")
    shaped = terms.reshape(terms.shape[0], far * core * near, terms.shape[1] // (far * core * near))
    return lax.dynamic_index_in_dim(shaped, slot, 1, keepdims=False)


def body(
    hidden_in,
    w_query,
    w_key,
    w_value,
    w_output,
    w_up,
    w_down,
    norm_gain,
    norm_bias,
    grad_out,
    group_id,
    group_scale,
    span_place,
):
    far, core, near = sizes()
    slot_index = (lax.axis_index("far") * core + lax.axis_index("core")) * near + lax.axis_index("fsdp")
    sources = slot_index // SPANS * SPANS + jnp.arange(SPANS, dtype=jnp.int32)
    slot_ids = jnp.arange(span_place.shape[0], dtype=jnp.int32)
    places = jnp.sum(jnp.where(sources[:, None] == slot_ids[None, :], span_place[None, :], 0), axis=1)
    own_place = jnp.sum(jnp.where(slot_ids == slot_index, span_place, 0))
    tables = turning_tables(SPANS * TOK_DEV)
    cosine, sine = [lax.dynamic_index_in_dim(t, own_place, 0, keepdims=False) for t in tables]

    side = lambda parts: jnp.concatenate(parts, axis=1)
    whole = lambda part: lax.all_gather(part, ("far", "core", "fsdp"), axis=0, tiled=True)
    three = lambda joined: [(joined, 0), (joined, SPANS), (joined, 2 * SPANS)]
    small = jnp.concatenate([norm_gain, norm_bias], axis=1)
    vector_count = small.shape[0] * small.shape[1]
    small = small.reshape(vector_count, small.shape[2]).T
    small = jnp.pad(small, ((0, 0), (0, 128 - vector_count)))
    down = Gather(w_down[0], False)
    late_up, late_down = (Gather(w_up[1], True), Gather(w_down[1], False))
    stages = len(down.order)

    first = whole(side([w_query[0], w_key[0], w_value[0], w_output[0], small]))
    begun = down.run(stages - 2)
    first, down.part = lax.optimization_barrier((first, begun))
    up_full = whole(w_up[0])
    second = whole(side([w_query[1], w_key[1], w_value[1], w_output[1]]))
    vectors = first[:, 4 * w_query.shape[2] :][:, :vector_count].T.astype(jnp.float32)
    vectors = vectors.reshape(2, 8, vectors.shape[1])

    def move(main, *gathers):
        main, parts = lax.optimization_barrier((main, [gather.run(1) for gather in gathers]))
        for gather, part in zip(gathers, parts):
            gather.part = part
        return main

    def forward_layer(layer, hidden, joined, moves, rest):
        normed, sent = project_in(hidden, vectors[layer], cosine, sine, three(joined))
        sent = list(move(list(sent), *moves[0]))
        pieces = [exchange(sent[0])]
        pieces[0] = move(pieces[0], *moves[1])
        pieces.append(exchange(sent[1]))
        attended, totals, back = ([], [], [])
        for pair in range(PAIRS):
            outs, total = attend(places, pieces[pair])
            if pair == 0:
                outs, pieces[1] = move((outs, pieces[1]), *moves[2])
            else:
                outs = move(outs, *moves[3])
            attended.append(outs)
            totals.append(total)
            back.append(exchange(outs))
        back = move(back, *moves[4])
        weights = rest()
        joined_heads, u, h, c, f, slope, m, y = feed(back, hidden, vectors[layer], *weights)
        y = move(y, *moves[5])
        kept = (hidden, normed, pieces, attended, totals, joined_heads, u, h, c, f, slope, m, joined, weights)
        return (y, kept)

    both = (late_up, late_down)
    hidden_mid, kept_first = forward_layer(
        0,
        hidden_in,
        first,
        [(), (), both, (down, *both), (down,), both],
        lambda: ((first, 3), up_full, down.part),
    )
    hidden_out, kept_second = forward_layer(
        1,
        hidden_mid,
        second,
        [(), (), both, both, (), ()],
        lambda: ((second, 3), late_up.run(), late_down.run()),
    )

    row_index = slot_index // SPANS
    row_ids = jnp.arange(group_id.shape[0], dtype=jnp.int32)
    group_of_row = jnp.sum(jnp.where(row_ids == row_index, group_id, 0))
    group_ids = jnp.arange(group_scale.shape[0], dtype=jnp.int32)
    row_scale = jnp.sum(jnp.where(group_ids == group_of_row, group_scale, 0.0))
    grad = grad_out.astype(jnp.float32) * row_scale

    def backward_layer(layer, grad, kept, points, late=None):
        hidden, normed, pieces, attended, totals, joined_heads, u, h, c, f, slope, m, joined, weights = kept
        output_weight, up_weight, down_weight = weights
        made, there = feed_back(
            grad, m, h, u, vectors[layer], output_weight, slope, down_weight, up_weight
        )
        gm, gz, grad_middle, gu, sums = made
        outer = Reduction([(c, gz), (f, gm), (joined_heads, gu)])
        there[0] = exchange(there[0])
        there = points[0](there, outer)
        there[1] = exchange(there[1])
        outer.swap()
        outs = attend_back(places, pieces[0], there[0], attended[0], *tables, totals[0])
        outer.join()
        outs, there = points[1]((outs, there), outer)
        outer.near(True)
        grads = [exchange(outs)]
        outs = attend_back(places, pieces[1], there[1], attended[1], *tables, totals[1])
        outs, grads = points[2]((outs, grads))
        grads.append(exchange(outs))
        grads = late(grads, outer) if late else points[3](grads)
        grad_in, more, joined_grad = project_back(
            grads, hidden, vectors[layer], grad_middle, three(joined)
        )
        inner = Reduction([(normed, joined_grad)])
        grad_in = tie(grad_in, inner)
        inner.swap()
        inner.join()
        return (grad_in, sums + more, outer, inner)

    grad, sums_second, outer_second, inner_second = backward_layer(
        1,
        grad,
        kept_second,
        [lambda main, outer: tie(main, outer), lambda main, outer: tie(main, outer), lambda main: main, lambda main: main],
    )
    grad = tie(grad, inner_second)
    inner_second.near(False)

    def after_feed(main, outer):
        main = tie(main, inner_second, outer)
        inner_second.far()
        return main
    def after_pair(main, outer):
        main = tie(main, inner_second, outer, outer_second)
        outer_second.far()
        return main


    grad_in, sums_first, outer_first, inner_first = backward_layer(
        0,
        grad,
        kept_first,
        [after_feed, after_pair, lambda main: main, lambda main: main],
        lambda main, outer: (tie(main, outer_second, outer), outer.far())[0],
    )
    inner_first.near(False)
    inner_first.far()
    vector_terms = sum_vectors(jnp.concatenate([sums_first, sums_second], axis=0))
    vector_terms = vector_terms.reshape(2, 2, 4, vector_terms.shape[1])
    up_pair, down_pair, output_pair = zip(outer_first.result(), outer_second.result())
    joined_pair = jnp.stack([inner_first.result()[0], inner_second.result()[0]])
    width = hidden_in.shape[1]
    return (
        hidden_mid,
        hidden_out,
        grad_in,
        joined_pair[:, :, :width],
        joined_pair[:, :, width : 2 * width],
        joined_pair[:, :, 2 * width :],
        jnp.stack(output_pair),
        jnp.stack(up_pair),
        jnp.stack(down_pair),
        vector_terms[:, 0],
        vector_terms[:, 1],
    )


def solution(mesh):
    count, near = mesh.devices.shape
    mesh = Mesh(mesh.devices.reshape(count // 2, 2, near), ("far", "core", "fsdp"))
    placed = (
        P(("far", "core", "fsdp"), None),
        P(None, ("far", "core", "fsdp"), None),
        P(None, ("far", "core", "fsdp"), None),
        P(None, ("far", "core", "fsdp"), None),
        P(None, ("far", "core", "fsdp"), None),
        P(None, ("far", "core", "fsdp"), None),
        P(None, ("far", "core", "fsdp"), None),
        P(None, None, ("far", "core", "fsdp")),
        P(None, None, ("far", "core", "fsdp")),
        P(("far", "core", "fsdp"), None),
        P(),
        P(),
        P(),
    )
    return jax.shard_map(
        body,
        mesh=mesh,
        in_specs=placed,
        out_specs=(
            P(("far", "core", "fsdp"), None),
            P(("far", "core", "fsdp"), None),
            P(("far", "core", "fsdp"), None),
            P(None, ("far", "core", "fsdp"), None),
            P(None, ("far", "core", "fsdp"), None),
            P(None, ("far", "core", "fsdp"), None),
            P(None, ("far", "core", "fsdp"), None),
            P(None, ("far", "core", "fsdp"), None),
            P(None, ("far", "core", "fsdp"), None),
            P(None, None, ("far", "core", "fsdp")),
            P(None, None, ("far", "core", "fsdp")),
        ),
        check_vma=False,
    )
```

```python
import functools
import math

import jax
import jax.numpy as jnp
from jax import lax
from jax.experimental import pallas as pl
from jax.experimental.pallas import tpu as pltpu
from jax.sharding import Mesh
from jax.sharding import PartitionSpec as P

HEAD_DIM = 64
TOK_DEV = 512
VMEM = 60 << 20
SPANS = 4


masked_score = -1e30
score_factor = 0.125


def product_rows(left, right):
    return lax.dot_general(
        left, right, (((0,), (0,)), ((), ())), preferred_element_type=jnp.float32
    )


NT = (((1,), (1,)), ((), ()))
NN = (((1,), (0,)), ((), ()))
TN = (((0,), (0,)), ((), ()))
PAIR = 2 * HEAD_DIM
PAIRS = 2


def mul(left, right, how):
    return lax.dot_general(left, right, how, preferred_element_type=jnp.float32)


def lane_in_head(parity, shape):
    lanes = lax.broadcasted_iota(jnp.int32, shape, 1)
    return (lanes // HEAD_DIM) == parity


def lasts(time):
    return pl.CostEstimate(flops=0, bytes_accessed=int(time * 1.7e6), transcendentals=0)


def whole_vmem():
    return pl.BlockSpec(memory_space=pltpu.VMEM)


def attend_kernel(places, pieces, outs, lse_ref, row, keys, values, scores, turned):
    head, block = pl.program_id(0), pl.program_id(1)
    span, width = outs.shape[1:]

    @pl.when((head == 0) & (block == 0))
    def _():
        for at in range(SPANS):
            row[places[at]] = pieces[at, :, :width] * score_factor
            keys[places[at]] = pieces[at, :, width : 2 * width]
            values[places[at]] = pieces[at, :, 2 * width :]

    parity = head % 2
    lanes = pl.ds(pl.multiple_of((head // 2) * PAIR, PAIR), PAIR)
    inside = lane_in_head(parity, (span, PAIR))
    queries = row[block, :, lanes]
    queries = jnp.where(inside, queries, jnp.zeros_like(queries))

    def first(at, highest):
        tile = mul(queries, keys[at, :, lanes], NT)
        scores[at] = tile
        for part in range(span // 128):
            highest = jnp.maximum(highest, tile[:, part * 128 : (part + 1) * 128])
        return highest

    highest = lax.fori_loop(0, block, first, jnp.full((span, 128), masked_score, jnp.float32))
    tile = mul(queries, keys[block, :, lanes], NT)
    later = lax.broadcasted_iota(jnp.int32, tile.shape, 1) > lax.broadcasted_iota(jnp.int32, tile.shape, 0)
    tile = jnp.where(later, masked_score, tile)
    scores[block] = tile
    for part in range(span // 128):
        highest = jnp.maximum(highest, tile[:, part * 128 : (part + 1) * 128])
    highest = jnp.max(highest, axis=1, keepdims=True)

    def second(at, total):
        weights = jnp.exp(scores[at] - highest).astype(jnp.bfloat16)
        extended = values[at, :, lanes]
        extended = jnp.where(inside, extended, jnp.ones_like(extended))
        return total + mul(weights, extended, NN)

    total = lax.fori_loop(0, block + 1, second, jnp.zeros((span, PAIR), jnp.float32))
    swapped = pltpu.roll(total, HEAD_DIM, 1)
    sums = jnp.where(inside, swapped, total)
    lse_ref[0, 0] = highest + jnp.log(sums)
    mine = (total / sums).astype(jnp.bfloat16)
    turned[block, :, lanes] = jnp.where(inside, mine, turned[block, :, lanes])

    @pl.when((head == pl.num_programs(0) - 1) & (block == SPANS - 1))
    def _():
        for at in range(SPANS):
            outs[at] = turned[places[at]]


def attend(places, pieces):
    _, span, triple = pieces.shape
    width = triple // 3
    heads = width // HEAD_DIM
    flops = heads * 20 * 2 * 2 * span * span * HEAD_DIM // 2
    return pl.pallas_call(
        attend_kernel,
        grid_spec=pltpu.PrefetchScalarGridSpec(
            num_scalar_prefetch=1,
            grid=(heads, SPANS),
            in_specs=[whole_vmem()],
            out_specs=[whole_vmem(), pl.BlockSpec((1, 1, span, PAIR), lambda h, b, p: (h, b, 0, 0))],
            scratch_shapes=[pltpu.VMEM((SPANS, span, width), jnp.bfloat16)] * 3
            + [
                pltpu.VMEM((SPANS, span, span), jnp.float32),
                pltpu.VMEM((SPANS, span, width), jnp.bfloat16),
            ],
        ),
        out_shape=[
            jax.ShapeDtypeStruct((SPANS, span, width), jnp.bfloat16),
            jax.ShapeDtypeStruct((heads, SPANS, span, PAIR), jnp.float32),
        ],
        compiler_params=pltpu.CompilerParams(vmem_limit_bytes=VMEM),
        cost_estimate=lasts(18),
        name="attend",
    )(places, pieces)


def other_half(values):
    half = HEAD_DIM // 2
    size = values.shape[1]
    lanes = lax.broadcasted_iota(jnp.int32, values.shape, 1)
    return jnp.where(
        lanes % HEAD_DIM < half, pltpu.roll(values, size - half, 1), pltpu.roll(values, half, 1)
    )


def turn(values, cosine, sine):
    return values * cosine + other_half(values) * sine


def turn_back(values, cosine, sine):
    return values * cosine - other_half(values) * sine


def attend_back_kernel(places, pieces, grads, attended, cosine_ref, sine_ref, lse_ref, outs, *held):
    row, keys, values, back, ahead, grad_q, grad_k, grad_v = held
    head, block = pl.program_id(0), pl.program_id(1)
    span, width = grads.shape[1:]

    @pl.when((head == 0) & (block == 0))
    def _():
        for at in range(SPANS):
            row[places[at]] = pieces[at, :, :width] * score_factor
            keys[places[at]] = pieces[at, :, width : 2 * width]
            values[places[at]] = pieces[at, :, 2 * width :]
            back[places[at]] = grads[at]
            ahead[places[at]] = attended[at]
        grad_q[...] = jnp.zeros_like(grad_q)
        grad_k[...] = jnp.zeros_like(grad_k)
        grad_v[...] = jnp.zeros_like(grad_v)

    parity = head % 2
    lanes = pl.ds(pl.multiple_of((head // 2) * PAIR, PAIR), PAIR)
    inside = lane_in_head(parity, (span, PAIR))
    only = lambda value: jnp.where(inside, value, jnp.zeros_like(value))
    queries = only(row[block, :, lanes])
    grad_out = only(back[block, :, lanes])
    lse_row = jnp.transpose(lse_ref[0, 0])[:1]
    terms = grad_out.astype(jnp.float32) * ahead[block, :, lanes].astype(jnp.float32)
    terms_row = jnp.sum(jnp.transpose(terms), axis=0, keepdims=True)

    def tile(at, masked):
        key_tile = keys[at, :, lanes]
        scores = mul(key_tile, queries, NT) - lse_row
        if masked:
            later = lax.broadcasted_iota(jnp.int32, scores.shape, 0) > lax.broadcasted_iota(
                jnp.int32, scores.shape, 1
            )
            scores = jnp.where(later, masked_score, scores)
        weights = jnp.exp(scores)
        grad_weights = mul(values[at, :, lanes], grad_out, NT)
        grad_scores = (weights * (grad_weights - terms_row)).astype(jnp.bfloat16)
        grad_v[at, :, lanes] += mul(weights.astype(jnp.bfloat16), grad_out, NN)
        grad_k[at, :, lanes] += mul(grad_scores, queries, NN)
        return mul(grad_scores, only(key_tile), TN)

    total = lax.fori_loop(
        0, block, lambda at, total: total + tile(at, False), jnp.zeros((span, PAIR), jnp.float32)
    )
    grad_q[block, :, lanes] += total + tile(block, True)

    @pl.when((head == pl.num_programs(0) - 1) & (block == SPANS - 1))
    def _():
        for at in range(SPANS):
            place = places[at]
            cosine, sine = cosine_ref[place], sine_ref[place]
            for pair in range(width // PAIR):
                part = slice(pair * PAIR, (pair + 1) * PAIR)
                outs[at, :, pair * PAIR : (pair + 1) * PAIR] = turn_back(
                    grad_q[place, :, part] * score_factor, cosine, sine
                ).astype(jnp.bfloat16)
                outs[at, :, width + pair * PAIR : width + (pair + 1) * PAIR] = turn_back(
                    grad_k[place, :, part], cosine, sine
                ).astype(jnp.bfloat16)
            outs[at, :, 2 * width :] = grad_v[place].astype(jnp.bfloat16)


def attend_back(places, pieces, grads, attended, cosine, sine, lse):
    _, span, width = grads.shape
    heads = width // HEAD_DIM
    flops = heads * 20 * 2 * 5 * span * span * HEAD_DIM // 2
    stored = lambda kind: pltpu.VMEM((SPANS, span, width), kind)
    return pl.pallas_call(
        attend_back_kernel,
        grid_spec=pltpu.PrefetchScalarGridSpec(
            num_scalar_prefetch=1,
            grid=(heads, SPANS),
            in_specs=[whole_vmem()] * 5
            + [pl.BlockSpec((1, 1, span, PAIR), lambda h, b, p: (h, b, 0, 0))],
            out_specs=whole_vmem(),
            scratch_shapes=[stored(jnp.bfloat16)] * 5 + [stored(jnp.float32)] * 3,
        ),
        out_shape=jax.ShapeDtypeStruct((SPANS, span, 3 * width), jnp.bfloat16),
        compiler_params=pltpu.CompilerParams(vmem_limit_bytes=VMEM),
        cost_estimate=lasts(25),
        name="attend_back",
    )(places, pieces, grads, attended, cosine, sine, lse)


def turning_tables(count):
    half = HEAD_DIM // 2
    frequency = jnp.exp(jnp.arange(half, dtype=jnp.float32) * (-math.log(10000.0) / half))
    angles = jnp.arange(count, dtype=jnp.float32)[:, None] * frequency[None, :]
    cosine, sine = jnp.cos(angles), jnp.sin(angles)
    cosine = jnp.concatenate([cosine] * 4, axis=1)
    sine = jnp.concatenate([-sine, sine, -sine, sine], axis=1)
    shape = (count // TOK_DEV, TOK_DEV, PAIR)
    return (cosine.reshape(shape), sine.reshape(shape))


ROWS = 256
norm_epsilon = 1e-05


def row_loop(count, body, carry):
    size = min(ROWS, count)
    return lax.fori_loop(
        0, count // size, lambda i, c: body(pl.ds(pl.multiple_of(i * size, size), size), c), carry
    )


def normal(values):
    centred = values - jnp.mean(values, axis=-1, keepdims=True)
    inverse = lax.rsqrt(jnp.mean(centred * centred, axis=-1, keepdims=True) + norm_epsilon)
    return (centred * inverse, inverse)


def norm_back(values, grad, gain):
    shape, inverse = normal(values)
    inner = grad * gain
    result = inverse * (
        inner
        - jnp.mean(inner, axis=-1, keepdims=True)
        - shape * jnp.mean(inner * shape, axis=-1, keepdims=True)
    )
    return (
        result,
        jnp.sum(grad * shape, axis=0, keepdims=True),
        jnp.sum(grad, axis=0, keepdims=True),
    )


def fixed(shape):
    return pl.BlockSpec(shape, lambda i: (0,) * len(shape), pipeline_mode=pl.Buffered(1))


def output_spec(block, model):
    return pl.BlockSpec((model, model), lambda i: (0, block), pipeline_mode=pl.Buffered(1))


def project_in_kernel(x_ref, vec_ref, cos_ref, sin_ref, wq_ref, wk_ref, wv_ref, normed_ref, *outs):
    tokens = x_ref.shape[0]

    @pl.when(pl.program_id(0) == 0)
    def _():
        def body(rows, carry):
            shape, _ = normal(x_ref[rows, :].astype(jnp.float32))
            normed_ref[rows, :] = (shape * vec_ref[0:1, :] + vec_ref[4:5, :]).astype(jnp.bfloat16)
            return carry

        row_loop(tokens, body, 0)

    for at, weight_ref in enumerate((wq_ref, wk_ref, wv_ref)):
        made = mul(normed_ref[...], weight_ref[...], NN)
        for pair, out in enumerate(outs):
            part = made[:, pair * PAIR : (pair + 1) * PAIR]
            if at < 2:
                part = turn(part, cos_ref[...], sin_ref[...])
            out[0, :, at * PAIR : (at + 1) * PAIR] = part.astype(jnp.bfloat16)


def weight_spec(weight, first, model):
    return pl.BlockSpec((model, model // SPANS), lambda r: (0, first + r))


def project_in(x, vectors, cosine, sine, weights):
    tokens, model = x.shape
    piece = pl.BlockSpec((1, tokens, 3 * PAIR), lambda r: (r, 0, 0))
    result = pl.pallas_call(
        project_in_kernel,
        grid=(SPANS,),
        in_specs=[fixed(x.shape), fixed(vectors.shape), fixed(cosine.shape), fixed(sine.shape)]
        + [weight_spec(weight, first, model) for weight, first in weights],
        out_specs=[fixed((tokens, model))] + [piece] * PAIRS,
        out_shape=[jax.ShapeDtypeStruct((tokens, model), jnp.bfloat16)]
        + [jax.ShapeDtypeStruct((SPANS, tokens, 3 * PAIR), jnp.bfloat16)] * PAIRS,
        compiler_params=pltpu.CompilerParams(vmem_limit_bytes=VMEM),
        cost_estimate=lasts(10),
        name="project_in",
    )(x, vectors, cosine, sine, *[weight for weight, _ in weights])
    return (result[0], result[1:])


def project_back_kernel(*refs):
    pieces, refs = refs[:PAIRS], refs[PAIRS:]
    x_ref, vec_ref, gh_ref, wq_ref, wk_ref, wv_ref, gx_ref, sums_ref, joined_ref, total = refs
    step = pl.program_id(0)
    tokens, model = x_ref.shape
    width = wq_ref.shape[1]
    made = None
    for at, weight_ref in enumerate((wq_ref, wk_ref, wv_ref)):
        part = jnp.concatenate(
            [piece[0, :, at * PAIR : (at + 1) * PAIR] for piece in pieces], axis=1
        )
        first = at * model + step * width
        joined_ref[:, pl.ds(pl.multiple_of(first, width), width)] = part
        one = mul(part, weight_ref[...], NT)
        made = one if made is None else made + one

    @pl.when(step == 0)
    def _():
        total[...] = made

    @pl.when(step > 0)
    def _():
        total[...] += made

    @pl.when(step == SPANS - 1)
    def _():
        def body(rows, carry):
            back, gain, bias = norm_back(
                x_ref[rows, :].astype(jnp.float32), total[rows, :], vec_ref[0:1, :]
            )
            gx_ref[rows, :] = gh_ref[rows, :] + back
            return (carry[0] + gain, carry[1] + bias)

        zero = jnp.zeros((1, model), jnp.float32)
        gain, bias = row_loop(tokens, body, (zero, zero))
        sums_ref[...] = jnp.zeros_like(sums_ref)
        sums_ref[0:1, :] = gain
        sums_ref[4:5, :] = bias


def project_back(pieces, x, vectors, grad_middle, weights):
    tokens, model = x.shape
    return pl.pallas_call(
        project_back_kernel,
        grid=(SPANS,),
        in_specs=[pl.BlockSpec((1, tokens, 3 * PAIR), lambda r: (r, 0, 0))] * PAIRS
        + [fixed(x.shape), fixed(vectors.shape), fixed(x.shape)]
        + [weight_spec(weight, first, model) for weight, first in weights],
        out_specs=[fixed(x.shape), fixed((8, model)), fixed((tokens, 3 * model))],
        scratch_shapes=[pltpu.VMEM((tokens, model), jnp.float32)],
        out_shape=[
            jax.ShapeDtypeStruct((tokens, model), jnp.float32),
            jax.ShapeDtypeStruct((8, model), jnp.float32),
            jax.ShapeDtypeStruct((tokens, 3 * model), jnp.bfloat16),
        ],
        compiler_params=pltpu.CompilerParams(vmem_limit_bytes=VMEM),
        cost_estimate=lasts(13),
        name="project_back",
    )(*pieces, x, vectors, grad_middle, *[weight for weight, _ in weights])


def gelu_parts(z):
    root = math.sqrt(2.0 / math.pi)
    square = z * z
    bent = jnp.tanh(root * z * (1.0 + 0.044715 * square))
    half = 0.5 * (1.0 + bent)
    slope = half + 0.5 * z * (1.0 - bent * bent) * (root * (1.0 + 3.0 * 0.044715 * square))
    return (z * half, slope)


FF_TILE = 1024
FOLD = 32


def unfold(folded, flat=None):
    if flat is None:
        return folded
    count, columns = flat.shape
    times = folded.shape[1] // columns
    for slot in range(folded.shape[0] // FOLD):
        for at in range(times):
            flat[(slot * times + at) * FOLD : (slot * times + at + 1) * FOLD, :] = folded[
                slot * FOLD : (slot + 1) * FOLD, at * columns : (at + 1) * columns
            ]
    return flat


def down_specs(weight, model, hidden):
    array, block = weight
    if array.shape == (hidden, model):
        return (pl.BlockSpec((FF_TILE, model), lambda i: (i, 0)), [])
    rows = FF_TILE * model // hidden
    return (
        pl.BlockSpec((rows, hidden), lambda i: (i, block)),
        [pltpu.VMEM((FF_TILE, model), jnp.bfloat16)],
    )


def feed_kernel(*refs):
    pieces, refs = refs[:PAIRS], refs[PAIRS:]
    x_ref, vec_ref, wo_ref, up_ref, down_ref = refs[:5]
    joined_ref, u_ref, h_ref, c_ref, f_ref, slope_ref, m_ref, y_ref = refs[5:13]
    flat = refs[13:]
    down_ref = unfold(down_ref, *flat)
    step = pl.program_id(0)
    tokens = x_ref.shape[0]

    @pl.when(step == 0)
    def _():
        for pair in range(PAIRS):
            for at in range(SPANS):
                first = (at * PAIRS + pair) * PAIR
                joined_ref[:, first : first + PAIR] = pieces[pair][at]
        u_ref[...] = mul(joined_ref[...], wo_ref[...], NN)

        def body(rows, carry):
            shape, _ = normal(u_ref[rows, :])
            middle = x_ref[rows, :].astype(jnp.float32) + shape * vec_ref[1:2, :] + vec_ref[5:6, :]
            h_ref[rows, :] = middle
            shape, _ = normal(middle)
            c_ref[rows, :] = (shape * vec_ref[2:3, :] + vec_ref[6:7, :]).astype(jnp.bfloat16)
            return carry

        row_loop(tokens, body, 0)

    @pl.when(step == 0)
    def _():
        m_ref[...] = jnp.zeros_like(m_ref)

    made, slope = gelu_parts(mul(c_ref[...], up_ref[...], NN))
    slope_ref[...] = slope.astype(jnp.bfloat16)
    made = made.astype(jnp.bfloat16)
    f_ref[...] = made
    m_ref[...] += mul(made, down_ref[...], NN)

    @pl.when(step == pl.num_programs(0) - 1)
    def _():
        def body(rows, carry):
            shape, _ = normal(m_ref[rows, :])
            result = h_ref[rows, :] + shape * vec_ref[3:4, :] + vec_ref[7:8, :]
            y_ref[rows, :] = result.astype(jnp.bfloat16)
            return carry

        row_loop(tokens, body, 0)


def feed(pieces, x, vectors, output_weight, up_weight, down_weight):
    tokens, model = x.shape
    hidden = 4 * model
    full = lambda kind, columns=model: jax.ShapeDtypeStruct((tokens, columns), kind)
    wide = pl.BlockSpec((tokens, FF_TILE), lambda i: (0, i))
    down_spec, flat = down_specs(down_weight, model, hidden)
    return pl.pallas_call(
        feed_kernel,
        grid=(hidden // FF_TILE,),
        in_specs=[fixed((SPANS, tokens, PAIR))] * PAIRS
        + [fixed(x.shape), fixed(vectors.shape), output_spec(output_weight[1], model)]
        + [
            pl.BlockSpec((model, FF_TILE), lambda i: (0, i)),
            down_spec,
        ],
        out_specs=[fixed(x.shape)] * 4 + [wide, wide] + [fixed(x.shape)] * 2,
        scratch_shapes=flat,
        out_shape=[
            full(jnp.bfloat16),
            full(jnp.float32),
            full(jnp.float32),
            full(jnp.bfloat16),
            full(jnp.bfloat16, hidden),
            full(jnp.bfloat16, hidden),
            full(jnp.float32),
            full(jnp.bfloat16),
        ],
        compiler_params=pltpu.CompilerParams(vmem_limit_bytes=VMEM),
        cost_estimate=lasts(24),
        name="feed",
    )(*pieces, x, vectors, output_weight[0], up_weight, down_weight[0])


def feed_back_kernel(*refs):
    gy_ref, m_ref, h_ref, u_ref, vec_ref, wo_ref, slope_ref, down_ref, up_ref = refs[:9]
    gm_ref, gz_ref, gh_ref, gu_ref, sums_ref = refs[9:14]
    pieces = refs[14 : 14 + PAIRS]
    total, back, *flat = refs[14 + PAIRS :]
    down_ref = unfold(down_ref, *flat)
    step = pl.program_id(0)
    tokens, model = gy_ref.shape
    zero = jnp.zeros((1, model), jnp.float32)

    @pl.when(step == 0)
    def _():
        def body(rows, carry):
            grad, gain, bias = norm_back(m_ref[rows, :], gy_ref[rows, :], vec_ref[3:4, :])
            gm_ref[rows, :] = grad.astype(jnp.bfloat16)
            return (carry[0] + gain, carry[1] + bias)

        gain, bias = row_loop(tokens, body, (zero, zero))
        sums_ref[0:1, :] = zero
        sums_ref[4:5, :] = zero
        sums_ref[3:4, :] = gain
        sums_ref[7:8, :] = bias

    @pl.when(step == 0)
    def _():
        total[...] = jnp.zeros_like(total)

    made = mul(gm_ref[...], down_ref[...], NT) * slope_ref[...].astype(jnp.float32)
    made = made.astype(jnp.bfloat16)
    gz_ref[...] = made
    total[...] += mul(made, up_ref[...], NT)

    @pl.when(step == pl.num_programs(0) - 1)
    def _():
        def body(rows, carry):
            grad, gain_two, bias_two = norm_back(h_ref[rows, :], total[rows, :], vec_ref[2:3, :])
            middle = gy_ref[rows, :] + grad
            gh_ref[rows, :] = middle
            grad, gain_one, bias_one = norm_back(u_ref[rows, :], middle, vec_ref[1:2, :])
            gu_ref[rows, :] = grad.astype(jnp.bfloat16)
            new = (gain_one, gain_two, bias_one, bias_two)
            return tuple(old + more for old, more in zip(carry, new))

        gain_one, gain_two, bias_one, bias_two = row_loop(tokens, body, (zero,) * 4)
        sums_ref[1:2, :] = gain_one
        sums_ref[2:3, :] = gain_two
        sums_ref[5:6, :] = bias_one
        sums_ref[6:7, :] = bias_two
        back[...] = mul(gu_ref[...], wo_ref[...], NT).astype(jnp.bfloat16)
        for pair in range(PAIRS):
            for at in range(SPANS):
                first = (at * PAIRS + pair) * PAIR
                pieces[pair][at] = back[:, first : first + PAIR]


def feed_back(grad, m, h, u, vectors, output_weight, slope, down_weight, up_weight):
    tokens, model = grad.shape
    hidden = 4 * model
    full = lambda kind, columns=model: jax.ShapeDtypeStruct((tokens, columns), kind)
    wide = pl.BlockSpec((tokens, FF_TILE), lambda i: (0, i))
    down_spec, flat = down_specs(down_weight, model, hidden)
    result = pl.pallas_call(
        feed_back_kernel,
        grid=(hidden // FF_TILE,),
        in_specs=[fixed(grad.shape)] * 4
        + [fixed(vectors.shape), output_spec(output_weight[1], model), wide]
        + [
            down_spec,
            pl.BlockSpec((model, FF_TILE), lambda i: (0, i)),
        ],
        out_specs=[fixed(grad.shape), wide, fixed(grad.shape), fixed(grad.shape)]
        + [fixed((8, model))]
        + [fixed((SPANS, tokens, PAIR))] * PAIRS,
        scratch_shapes=[
            pltpu.VMEM((tokens, model), jnp.float32),
            pltpu.VMEM((tokens, model), jnp.bfloat16),
            *flat,
        ],
        out_shape=[
            full(jnp.bfloat16),
            full(jnp.bfloat16, hidden),
            full(jnp.float32),
            full(jnp.bfloat16),
            jax.ShapeDtypeStruct((8, model), jnp.float32),
        ]
        + [jax.ShapeDtypeStruct((SPANS, tokens, PAIR), jnp.bfloat16)] * PAIRS,
        compiler_params=pltpu.CompilerParams(vmem_limit_bytes=VMEM),
        cost_estimate=lasts(26),
        name="feed_back",
    )(grad, m, h, u, vectors, output_weight[0], slope, down_weight[0], up_weight)
    return (result[:5], list(result[5:]))


def weave_kernel(mine, own_ref, other_ref, out_ref):
    count = own_ref.shape[1]
    first = pl.multiple_of(mine[0] * count, count)
    second = pl.multiple_of((1 - mine[0]) * count, count)
    out_ref[0, pl.ds(first, count), :] = own_ref[0]
    out_ref[0, pl.ds(second, count), :] = other_ref[0]


def weave(own, other, mine):
    outer, count, columns = own.shape
    if count % 16 or columns % 128:
        return jnp.where(
            mine == 0, jnp.concatenate([own, other], axis=1), jnp.concatenate([other, own], axis=1)
        )
    spec = pl.BlockSpec((1, count, columns), lambda i, s: (i, 0, 0))
    return pl.pallas_call(
        weave_kernel,
        grid_spec=pltpu.PrefetchScalarGridSpec(
            num_scalar_prefetch=1,
            grid=(outer,),
            in_specs=[spec, spec],
            out_specs=pl.BlockSpec((1, 2 * count, columns), lambda i, s: (i, 0, 0)),
        ),
        out_shape=jax.ShapeDtypeStruct((outer, 2 * count, columns), own.dtype),
        compiler_params=pltpu.CompilerParams(vmem_limit_bytes=VMEM),
        cost_estimate=lasts(3),
        name="weave",
    )(jnp.reshape(mine, (1,)), own, other)


def half_kernel(which, *refs, far, near, start):
    lefts, (right_ref, *more, out_ref, turned) = refs[:far], refs[far:]

    @pl.when(pl.program_id(0) == 0)
    def _():
        for at, left_ref in enumerate(lefts):
            size = left_ref.shape[1]
            turned[at * size : (at + 1) * size, :] = jnp.transpose(left_ref[...])

    made = mul(turned[...], right_ref[...], NN)
    if not more:
        out_ref[...] = made.astype(out_ref.dtype)
        return
    made = (made + more[0][...].astype(jnp.float32)).astype(out_ref.dtype)
    rows = out_ref.shape[2]
    for z in range(far):
        for f in range(near):
            at = (z * near + f) * rows
            out_ref[f, z] = made[at : at + rows]


def half_rows_kernel(which, left_ref, right_ref, *refs, near):
    out_ref = refs[-1]
    made = mul(left_ref[...], right_ref[...], TN)
    if len(refs) == 1:
        out_ref[...] = made.astype(out_ref.dtype)
        return
    made = (made + refs[0][...].astype(jnp.float32)).astype(out_ref.dtype)
    rows, columns = out_ref.shape[2], made.shape[1]
    for f in range(near):
        for q in range(out_ref.shape[3] // columns):
            at = f * (made.shape[0] // near) + q * rows
            out_ref[f, 0, :, q * columns : (q + 1) * columns] = made[at : at + rows]


def half_product(left, right, which, far, near, got=None, joint=None, start=0, width=0, rows=0):
    tokens, count = left.shape
    columns = right.shape[1]
    size = count // (2 * far)
    which = jnp.reshape(which, (1,))
    tall = size // near > rows if got is not None else count > columns
    tile = columns if tall else min(columns, 1024)
    if tall:
        grid = (far,)
        ins = [
            pl.BlockSpec((tokens, size), lambda i, w: (0, 2 * i + w[0])),
            pl.BlockSpec((tokens, columns), lambda i, w: (0, 0)),
        ]
        lefts, scratch = [left], []
        flat = pl.BlockSpec((size, columns), lambda i, w: (i, 0))
        wide = columns * (size // near // rows) if got is not None else 0
        spread = pl.BlockSpec((near, 1, rows, wide), lambda i, w: (0, i, 0, start // wide))
        kernel = functools.partial(half_rows_kernel, near=near)
    else:
        grid = (columns // tile,)
        ins = [
            pl.BlockSpec((tokens, size), lambda c, w, at=at: (0, 2 * at + w[0])) for at in range(far)
        ] + [pl.BlockSpec((tokens, tile), lambda c, w: (0, c))]
        lefts, scratch = [left] * far, [pltpu.VMEM((count // 2, tokens), jnp.bfloat16)]
        flat = pl.BlockSpec((count // 2, tile), lambda c, w: (0, c))
        spread = pl.BlockSpec((near, far, rows, tile), lambda c, w: (0, 0, 0, start // tile + c))
        kernel = functools.partial(half_kernel, far=far, near=near, start=start)
    operands, aliases = ([*lefts, right], {})
    if got is None:
        shape, out = (count // 2, columns), flat
    else:
        shape, out = (near, far, rows, width), spread
        operands.append(got)
        ins.append(flat)
        if joint is not None:
            plain = kernel
            kernel = lambda *refs: plain(*refs[: 1 + len(operands) - 1], *refs[1 + len(operands) :])
            operands.append(joint)
            ins.append(pl.BlockSpec(memory_space=pl.ANY))
            aliases = {len(operands): 0}
    return pl.pallas_call(
        kernel,
        grid_spec=pltpu.PrefetchScalarGridSpec(
            num_scalar_prefetch=1, grid=grid, in_specs=ins, out_specs=out, scratch_shapes=scratch
        ),
        out_shape=jax.ShapeDtypeStruct(shape, jnp.bfloat16),
        input_output_aliases=aliases,
        compiler_params=pltpu.CompilerParams(vmem_limit_bytes=VMEM),
        cost_estimate=lasts(6),
        name="half_product",
    )(which, *operands)


def sizes():
    return (lax.axis_size("far"), lax.axis_size("core"), lax.axis_size("fsdp"))


def flip(array, axis, apart):
    return lax.ppermute(array, axis, [(i, i ^ apart) for i in range(lax.axis_size(axis))])


def swap_cores(array):
    return flip(array, "core", 1)


def after(values, *others):
    return lax.optimization_barrier((values, others))[0]


def exchange(pieces):
    count = lax.axis_size("fsdp")
    rows = [list(range(at, at + SPANS)) for at in range(0, count, SPANS)]
    return lax.all_to_all(
        pieces, "fsdp", 0, 0, axis_index_groups=rows if len(rows) > 1 else None, tiled=True
    )


class Gather:
    def __init__(self, part, inner_first):
        far, _, near = sizes()
        steps = lambda axis, count: [(axis, i) for i in range(count.bit_length() - 1)]
        inner = steps("fsdp", near)
        if inner_first:
            inner = inner[1::-1] + inner[2:]
        self.part = part
        self.order = steps("far", far)[::-1] + inner + [("core", 0)]
        self.place = {bit: at for at, bit in enumerate(steps("fsdp", near) + [("core", 0)] + steps("far", far))}
        self.held = []

    def send(self):
        bit = self.order.pop(0)
        outer = 2 ** sum(1 for other in self.held if self.place[other] > self.place[bit])
        rows, columns = self.part.shape
        self.own = self.part.reshape(outer, rows // outer, columns)
        self.other = flip(self.own, bit[0], 1 << bit[1])
        self.mine = lax.axis_index(bit[0]) >> bit[1] & 1
        self.held.append(bit)

    def take(self, *others):
        own = after(self.own, *others) if others else self.own
        outer, rows, columns = own.shape
        self.part = weave(own, self.other, self.mine).reshape(2 * outer * rows, columns)

    def run(self, count=None):
        for _ in range(len(self.order) if count is None else count):
            self.send()
            self.take()
        return self.part


class Reduction:
    def __init__(self, products, vectors=None):
        self.products, self.vectors = products, vectors
        far, core, near = sizes()
        self.rows = products[0][0].shape[1] // (far * core * near)
        self.plain = self.rows % 16 != 0
        self.stage = 0
        self.value, self.apart = ((), 0)
        if not self.plain:
            self.value = [
                half_product(left, right, 1 - lax.axis_index("core"), far, near)
                for left, right in products
            ]
            if vectors is not None:
                turned = jnp.pad(vectors.T, ((0, 0), (0, 128 - vectors.shape[0])))
                halves = turned.reshape(far, core, near, self.rows, 128)
                pick = lambda at: lax.dynamic_index_in_dim(halves, at, 1, keepdims=False)
                mine = lax.axis_index("core")
                self.value.append(pick(1 - mine))
                self.vectors = pick(mine)

    def swap(self):
        if not self.plain:
            self.got = [swap_cores(value) for value in self.value]
            self.value = ()

    def join(self):
        if self.plain:
            return
        far, core, near = sizes()
        block = self.rows * far * near
        extra = None
        if self.vectors is not None:
            extra = (self.vectors + self.got.pop()).astype(jnp.bfloat16).transpose(1, 0, 2, 3)
        width = sum(value.size for value in self.got) // block
        width += 0 if extra is None else 128
        joint, start = None, 0
        for (left, right), got in zip(self.products, self.got):
            joint = half_product(
                left, right, lax.axis_index("core"), far, near, got, joint, start, width, self.rows
            )
            start += got.size // block
        if extra is not None:
            joint = lax.dynamic_update_slice_in_dim(joint, extra, start, axis=3)
        self.value = joint

    def near(self, offload):
        if self.plain:
            return
        count, far, rows, width = self.value.shape
        flat = self.value.reshape(count * far * rows, width)
        if offload:
            self.value = lax.psum_scatter(flat, "fsdp", scatter_dimension=0, tiled=True)
        else:
            self.got = lax.all_to_all(flat, "fsdp", 0, 0, tiled=True).reshape(count, far * rows, width)

    def near_take(self, *others):
        if self.plain:
            return
        got = after(self.got, *others) if others else self.got
        self.value = jnp.sum(got.astype(jnp.float32), axis=0).astype(jnp.bfloat16)

    def send(self):
        if self.plain:
            return
        if self.apart == 0:
            self.value = self.value.reshape(-1, self.rows, self.value.shape[-1])
            self.apart = 1
        mine = lax.axis_index("far") // self.apart % 2
        split = self.value.reshape(self.value.shape[0] // 2, 2, *self.value.shape[1:])
        pick = lambda at: lax.dynamic_index_in_dim(split, at, 1, keepdims=False)
        self.got = flip(pick(1 - mine), "far", self.apart)
        self.value = pick(mine)
        self.apart *= 2

    def take(self, *others):
        if self.plain:
            return
        kept = after(self.value, *others) if others else self.value
        value = kept.astype(jnp.float32) + self.got.astype(jnp.float32)
        self.value = value.astype(jnp.bfloat16) if value.shape[0] > 1 else value

    def rest(self):
        while not self.plain and self.value.shape[0] > 1:
            self.send()
            self.take()

    def result(self):
        if self.plain:
            sums = [
                lax.psum_scatter(
                    product_rows(left, right), ("far", "core", "fsdp"), scatter_dimension=0, tiled=True
                )
                for left, right in self.products
            ]
            if self.vectors is not None:
                axes = ("far", "core", "fsdp")
                sums.append(lax.psum_scatter(self.vectors, axes, scatter_dimension=1, tiled=True))
            return sums
        total = jnp.sum(self.value.astype(jnp.float32), axis=0)
        sums, first = ([], 0)
        for left, right in self.products:
            count = left.shape[1] // self.products[0][0].shape[1]
            columns = right.shape[1]
            part = total[:, first : first + count * columns]
            part = part.reshape(self.rows, count, columns).transpose(1, 0, 2)
            sums.append(part.reshape(count * self.rows, columns))
            first += count * columns
        if self.vectors is not None:
            sums.append(total[:, first:])
        return sums


def tie(main, *reductions):
    main, values = lax.optimization_barrier((main, [reduction.value for reduction in reductions]))
    for reduction, value in zip(reductions, values):
        reduction.value = value
    return main


def body(
    hidden_in,
    w_query,
    w_key,
    w_value,
    w_output,
    w_up,
    w_down,
    norm_gain,
    norm_bias,
    grad_out,
    group_id,
    group_scale,
    span_place,
):
    far, core, near = sizes()
    slot_index = (lax.axis_index("far") * core + lax.axis_index("core")) * near + lax.axis_index("fsdp")
    sources = slot_index // SPANS * SPANS + jnp.arange(SPANS, dtype=jnp.int32)
    slot_ids = jnp.arange(span_place.shape[0], dtype=jnp.int32)
    places = jnp.sum(jnp.where(sources[:, None] == slot_ids[None, :], span_place[None, :], 0), axis=1)
    own_place = jnp.sum(jnp.where(slot_ids == slot_index, span_place, 0))
    tables = turning_tables(SPANS * TOK_DEV)
    cosine, sine = [lax.dynamic_index_in_dim(t, own_place, 0, keepdims=False) for t in tables]

    side = lambda parts: jnp.concatenate(parts, axis=1)
    whole = lambda part: lax.all_gather(part, ("far", "core", "fsdp"), axis=0, tiled=True)
    small = jnp.concatenate([norm_gain, norm_bias], axis=1)
    vector_count = small.shape[0] * small.shape[1]
    small = small.reshape(vector_count, small.shape[2]).T
    small = jnp.pad(small, ((0, 0), (0, 128 - vector_count)))
    query_key = Gather(side([w_query[1], w_key[1]]), False)
    value_output = Gather(side([w_value[1], w_output[1]]), True)
    late = (query_key, value_output)
    begun = [gather.run(3) for gather in late]
    folds = w_up.shape[1] % FOLD == 0

    def gather_outer(layer):
        up_part, down_part = w_up[layer], w_down[layer]
        if not folds:
            return (whole(up_part), (whole(down_part), 0))
        rows, columns = up_part.shape
        folded = down_part.reshape(columns // down_part.shape[1], rows, down_part.shape[1])
        folded = folded.transpose(1, 0, 2).reshape(rows, columns)
        joint = whole(side([up_part, folded]))
        return (joint, (joint, 1))

    first = whole(side([w_query[0], w_key[0], w_value[0], w_output[0], small]))
    outer_first_weights, outer_second_weights = (gather_outer(0), gather_outer(1))
    vectors = first[:, 4 * w_query.shape[2] :][:, :vector_count].T.astype(jnp.float32)
    vectors = vectors.reshape(2, 8, vectors.shape[1])

    def forward_layer(layer, hidden, joined, begin, middle, rest):
        normed, sent = project_in(hidden, vectors[layer], cosine, sine, joined)
        sent = begin(list(sent))
        pieces = [exchange(sent[0])]
        pieces.append(exchange(sent[1]))
        attended, totals, back = ([], [], [])
        for pair in range(PAIRS):
            outs, total = attend(places, pieces[pair])
            if pair == 0:
                outs, pieces[1] = lax.optimization_barrier((outs, pieces[1]))
            attended.append(outs)
            totals.append(total)
            back.append(exchange(outs))
        middle(outs)
        joined_heads, u, h, c, f, slope, m, y = feed(back, hidden, vectors[layer], *rest)
        kept = (hidden, normed, pieces, attended, totals, joined_heads, u, h, c, f, slope, m, joined, rest)
        return (y, kept)

    def begin_late(sent):
        sent, begun_parts = lax.optimization_barrier((sent, begun))
        for gather, part in zip(late, begun_parts):
            gather.part = part
            gather.send()
        return sent

    def take_late(outs):
        for gather in late:
            gather.take(outs)
            gather.send()

    hidden_mid, kept_first = forward_layer(
        0,
        hidden_in,
        [(first, 0), (first, SPANS), (first, 2 * SPANS)],
        begin_late,
        take_late,
        ((first, 3), *outer_first_weights),
    )
    for gather in late:
        gather.take(hidden_mid)
        gather.run()
    hidden_out, kept_second = forward_layer(
        1,
        hidden_mid,
        [(query_key.part, 0), (query_key.part, SPANS), (value_output.part, 0)],
        lambda sent: sent,
        lambda outs: None,
        ((value_output.part, 1), *outer_second_weights),
    )

    row_index = slot_index // SPANS
    row_ids = jnp.arange(group_id.shape[0], dtype=jnp.int32)
    group_of_row = jnp.sum(jnp.where(row_ids == row_index, group_id, 0))
    group_ids = jnp.arange(group_scale.shape[0], dtype=jnp.int32)
    row_scale = jnp.sum(jnp.where(group_ids == group_of_row, group_scale, 0.0))
    grad = grad_out.astype(jnp.float32) * row_scale

    def backward_layer(layer, grad, kept, points, vector_terms=None):
        hidden, normed, pieces, attended, totals, joined_heads, u, h, c, f, slope, m, joined, weights = kept
        output_weight, up_weight, down_weight = weights
        made, there = feed_back(
            grad, m, h, u, vectors[layer], output_weight, slope, down_weight, up_weight
        )
        gm, gz, grad_middle, gu, sums = made
        outer = Reduction([(c, gz), (f, gm), (joined_heads, gu)])
        there[0] = exchange(there[0])
        there = points[0](there, outer)
        there[1] = exchange(there[1])
        outer.swap()
        outs = attend_back(places, pieces[0], there[0], attended[0], *tables, totals[0])
        outer.join()
        outs, there = points[1]((outs, there), outer)
        if layer == 0:
            outer.near(True)
        grads = [exchange(outs)]
        outs = attend_back(places, pieces[1], there[1], attended[1], *tables, totals[1])
        outs, grads = lax.optimization_barrier((outs, grads))
        points[2](outs)
        grads.append(exchange(outs))
        grads = points[4](grads, outer)
        if layer:
            outer.near(True)
        grad_in, more, joined_grad = project_back(
            grads, hidden, vectors[layer], grad_middle, joined
        )
        sums = sums + more
        if vector_terms is not None:
            vector_terms = jnp.concatenate([sums, vector_terms], axis=0)
        inner = Reduction([(normed, joined_grad)], vector_terms)
        grad_in = points[3](grad_in, inner)
        inner.swap()
        inner.join()
        return (grad_in, sums, outer, inner)

    grad, sums_second, outer_second, inner_second = backward_layer(
        1, grad, kept_second, [tie, tie, lambda outs: None, tie, tie]
    )
    grad = tie(grad, inner_second)

    def after_feed(main, outer):
        main = tie(main, inner_second, outer)
        inner_second.near(False)
        return main


    def after_pair(main, outer):
        inner_second.near_take(main)
        main = tie(main, outer, outer_second, inner_second)
        outer_second.send()
        inner_second.send()
        return main

    def after_pairs(outs):
        outer_second.take(outs)
        outer_second.send()
        inner_second.take(outs)
        inner_second.send()

    def after_return(grads, outer):
        outer_second.take()
        inner_second.take()
        return tie(grads, outer_second, inner_second)

    grad_in, _, outer_first, inner_first = backward_layer(
        0, grad, kept_first, [after_feed, after_pair, after_pairs, tie, after_return], sums_second
    )
    outer_first.value = after(outer_first.value, inner_first.value)
    inner_first.near(False)
    outer_first.send()
    outer_first.take()
    inner_first.near_take(outer_first.value)
    outer_first.rest()
    inner_first.rest()
    up_pair, down_pair, output_pair = zip(outer_first.result(), outer_second.result())
    joined_first, vector_terms = inner_first.result()
    if not inner_first.plain:
        vector_terms = vector_terms[:, :16].T
    vector_terms = vector_terms.reshape(2, 2, 4, vector_terms.shape[1])
    joined_pair = jnp.stack([joined_first, inner_second.result()[0]])
    width = hidden_in.shape[1]
    return (
        hidden_mid,
        hidden_out,
        grad_in,
        joined_pair[:, :, :width],
        joined_pair[:, :, width : 2 * width],
        joined_pair[:, :, 2 * width :],
        jnp.stack(output_pair),
        jnp.stack(up_pair),
        jnp.stack(down_pair),
        vector_terms[:, 0],
        vector_terms[:, 1],
    )


def solution(mesh):
    count, near = mesh.devices.shape
    mesh = Mesh(mesh.devices.reshape(count // 2, 2, near), ("far", "core", "fsdp"))
    placed = (
        P(("far", "core", "fsdp"), None),
        P(None, ("far", "core", "fsdp"), None),
        P(None, ("far", "core", "fsdp"), None),
        P(None, ("far", "core", "fsdp"), None),
        P(None, ("far", "core", "fsdp"), None),
        P(None, ("far", "core", "fsdp"), None),
        P(None, ("far", "core", "fsdp"), None),
        P(None, None, ("far", "core", "fsdp")),
        P(None, None, ("far", "core", "fsdp")),
        P(("far", "core", "fsdp"), None),
        P(),
        P(),
        P(),
    )
    return jax.shard_map(
        body,
        mesh=mesh,
        in_specs=placed,
        out_specs=(
            P(("far", "core", "fsdp"), None),
            P(("far", "core", "fsdp"), None),
            P(("far", "core", "fsdp"), None),
            P(None, ("far", "core", "fsdp"), None),
            P(None, ("far", "core", "fsdp"), None),
            P(None, ("far", "core", "fsdp"), None),
            P(None, ("far", "core", "fsdp"), None),
            P(None, ("far", "core", "fsdp"), None),
            P(None, ("far", "core", "fsdp"), None),
            P(None, None, ("far", "core", "fsdp")),
            P(None, None, ("far", "core", "fsdp")),
        ),
        check_vma=False,
    )
```

```python
import functools
import math

import jax
import jax.numpy as jnp
from jax import lax
from jax.experimental import pallas as pl
from jax.experimental.pallas import tpu as pltpu
from jax.sharding import Mesh
from jax.sharding import PartitionSpec as P

HEAD_DIM = 64
TOK_DEV = 512
VMEM = 60 << 20
SPANS = 4


masked_score = -1e30
score_factor = 0.125


def product_rows(left, right):
    return lax.dot_general(
        left, right, (((0,), (0,)), ((), ())), preferred_element_type=jnp.float32
    )


NT = (((1,), (1,)), ((), ()))
NN = (((1,), (0,)), ((), ()))
TN = (((0,), (0,)), ((), ()))
PAIR = 2 * HEAD_DIM
PAIRS = 2


def mul(left, right, how):
    return lax.dot_general(left, right, how, preferred_element_type=jnp.float32)


def lane_in_head(parity, shape):
    lanes = lax.broadcasted_iota(jnp.int32, shape, 1)
    return (lanes // HEAD_DIM) == parity


def lasts(time):
    return pl.CostEstimate(flops=0, bytes_accessed=int(time * 1.7e6), transcendentals=0)


def whole_vmem():
    return pl.BlockSpec(memory_space=pltpu.VMEM)


def attend_kernel(places, pieces, outs, lse_ref, row, keys, values, scores, turned):
    head, block = pl.program_id(0), pl.program_id(1)
    span, width = outs.shape[1:]

    @pl.when((head == 0) & (block == 0))
    def _():
        for at in range(SPANS):
            row[places[at]] = pieces[at, :, :width] * score_factor
            keys[places[at]] = pieces[at, :, width : 2 * width]
            values[places[at]] = pieces[at, :, 2 * width :]

    parity = head % 2
    lanes = pl.ds(pl.multiple_of((head // 2) * PAIR, PAIR), PAIR)
    inside = lane_in_head(parity, (span, PAIR))
    queries = row[block, :, lanes]
    queries = jnp.where(inside, queries, jnp.zeros_like(queries))

    def first(at, highest):
        tile = mul(queries, keys[at, :, lanes], NT)
        scores[at] = tile
        for part in range(span // 128):
            highest = jnp.maximum(highest, tile[:, part * 128 : (part + 1) * 128])
        return highest

    highest = lax.fori_loop(0, block, first, jnp.full((span, 128), masked_score, jnp.float32))
    tile = mul(queries, keys[block, :, lanes], NT)
    later = lax.broadcasted_iota(jnp.int32, tile.shape, 1) > lax.broadcasted_iota(jnp.int32, tile.shape, 0)
    tile = jnp.where(later, masked_score, tile)
    scores[block] = tile
    for part in range(span // 128):
        highest = jnp.maximum(highest, tile[:, part * 128 : (part + 1) * 128])
    highest = jnp.max(highest, axis=1, keepdims=True)

    def second(at, total):
        weights = jnp.exp(scores[at] - highest).astype(jnp.bfloat16)
        extended = values[at, :, lanes]
        extended = jnp.where(inside, extended, jnp.ones_like(extended))
        return total + mul(weights, extended, NN)

    total = lax.fori_loop(0, block + 1, second, jnp.zeros((span, PAIR), jnp.float32))
    swapped = pltpu.roll(total, HEAD_DIM, 1)
    sums = jnp.where(inside, swapped, total)
    lse_ref[0, 0] = highest + jnp.log(sums)
    mine = (total / sums).astype(jnp.bfloat16)
    turned[block, :, lanes] = jnp.where(inside, mine, turned[block, :, lanes])

    @pl.when((head == pl.num_programs(0) - 1) & (block == SPANS - 1))
    def _():
        for at in range(SPANS):
            outs[at] = turned[places[at]]


def attend(places, pieces):
    _, span, triple = pieces.shape
    width = triple // 3
    heads = width // HEAD_DIM
    flops = heads * 20 * 2 * 2 * span * span * HEAD_DIM // 2
    return pl.pallas_call(
        attend_kernel,
        grid_spec=pltpu.PrefetchScalarGridSpec(
            num_scalar_prefetch=1,
            grid=(heads, SPANS),
            in_specs=[whole_vmem()],
            out_specs=[whole_vmem(), pl.BlockSpec((1, 1, span, PAIR), lambda h, b, p: (h, b, 0, 0))],
            scratch_shapes=[pltpu.VMEM((SPANS, span, width), jnp.bfloat16)] * 3
            + [
                pltpu.VMEM((SPANS, span, span), jnp.float32),
                pltpu.VMEM((SPANS, span, width), jnp.bfloat16),
            ],
        ),
        out_shape=[
            jax.ShapeDtypeStruct((SPANS, span, width), jnp.bfloat16),
            jax.ShapeDtypeStruct((heads, SPANS, span, PAIR), jnp.float32),
        ],
        compiler_params=pltpu.CompilerParams(vmem_limit_bytes=VMEM),
        cost_estimate=lasts(18),
        name="attend",
    )(places, pieces)


def other_half(values):
    half = HEAD_DIM // 2
    size = values.shape[1]
    lanes = lax.broadcasted_iota(jnp.int32, values.shape, 1)
    return jnp.where(
        lanes % HEAD_DIM < half, pltpu.roll(values, size - half, 1), pltpu.roll(values, half, 1)
    )


def turn(values, cosine, sine):
    return values * cosine + other_half(values) * sine


def turn_back(values, cosine, sine):
    return values * cosine - other_half(values) * sine


def attend_back_kernel(places, pieces, grads, attended, cosine_ref, sine_ref, lse_ref, outs, *held):
    row, keys, values, back, ahead, grad_q, grad_k, grad_v = held
    head, block = pl.program_id(0), pl.program_id(1)
    span, width = grads.shape[1:]

    @pl.when((head == 0) & (block == 0))
    def _():
        for at in range(SPANS):
            row[places[at]] = pieces[at, :, :width] * score_factor
            keys[places[at]] = pieces[at, :, width : 2 * width]
            values[places[at]] = pieces[at, :, 2 * width :]
            back[places[at]] = grads[at]
            ahead[places[at]] = attended[at]
        grad_q[...] = jnp.zeros_like(grad_q)
        grad_k[...] = jnp.zeros_like(grad_k)
        grad_v[...] = jnp.zeros_like(grad_v)

    parity = head % 2
    lanes = pl.ds(pl.multiple_of((head // 2) * PAIR, PAIR), PAIR)
    inside = lane_in_head(parity, (span, PAIR))
    only = lambda value: jnp.where(inside, value, jnp.zeros_like(value))
    queries = only(row[block, :, lanes])
    grad_out = only(back[block, :, lanes])
    lse_row = jnp.transpose(lse_ref[0, 0])[:1]
    terms = grad_out.astype(jnp.float32) * ahead[block, :, lanes].astype(jnp.float32)
    terms_row = jnp.sum(jnp.transpose(terms), axis=0, keepdims=True)

    def tile(at, masked):
        key_tile = keys[at, :, lanes]
        scores = mul(key_tile, queries, NT) - lse_row
        if masked:
            later = lax.broadcasted_iota(jnp.int32, scores.shape, 0) > lax.broadcasted_iota(
                jnp.int32, scores.shape, 1
            )
            scores = jnp.where(later, masked_score, scores)
        weights = jnp.exp(scores)
        grad_weights = mul(values[at, :, lanes], grad_out, NT)
        grad_scores = (weights * (grad_weights - terms_row)).astype(jnp.bfloat16)
        grad_v[at, :, lanes] += mul(weights.astype(jnp.bfloat16), grad_out, NN)
        grad_k[at, :, lanes] += mul(grad_scores, queries, NN)
        return mul(grad_scores, only(key_tile), TN)

    total = lax.fori_loop(
        0, block, lambda at, total: total + tile(at, False), jnp.zeros((span, PAIR), jnp.float32)
    )
    grad_q[block, :, lanes] += total + tile(block, True)

    @pl.when((head == pl.num_programs(0) - 1) & (block == SPANS - 1))
    def _():
        for at in range(SPANS):
            place = places[at]
            cosine, sine = cosine_ref[place], sine_ref[place]
            for pair in range(width // PAIR):
                part = slice(pair * PAIR, (pair + 1) * PAIR)
                outs[at, :, pair * PAIR : (pair + 1) * PAIR] = turn_back(
                    grad_q[place, :, part] * score_factor, cosine, sine
                ).astype(jnp.bfloat16)
                outs[at, :, width + pair * PAIR : width + (pair + 1) * PAIR] = turn_back(
                    grad_k[place, :, part], cosine, sine
                ).astype(jnp.bfloat16)
            outs[at, :, 2 * width :] = grad_v[place].astype(jnp.bfloat16)


def attend_back(places, pieces, grads, attended, cosine, sine, lse):
    _, span, width = grads.shape
    heads = width // HEAD_DIM
    flops = heads * 20 * 2 * 5 * span * span * HEAD_DIM // 2
    stored = lambda kind: pltpu.VMEM((SPANS, span, width), kind)
    return pl.pallas_call(
        attend_back_kernel,
        grid_spec=pltpu.PrefetchScalarGridSpec(
            num_scalar_prefetch=1,
            grid=(heads, SPANS),
            in_specs=[whole_vmem()] * 5
            + [pl.BlockSpec((1, 1, span, PAIR), lambda h, b, p: (h, b, 0, 0))],
            out_specs=whole_vmem(),
            scratch_shapes=[stored(jnp.bfloat16)] * 5 + [stored(jnp.float32)] * 3,
        ),
        out_shape=jax.ShapeDtypeStruct((SPANS, span, 3 * width), jnp.bfloat16),
        compiler_params=pltpu.CompilerParams(vmem_limit_bytes=VMEM),
        cost_estimate=lasts(25),
        name="attend_back",
    )(places, pieces, grads, attended, cosine, sine, lse)


def turning_tables(count):
    half = HEAD_DIM // 2
    frequency = jnp.exp(jnp.arange(half, dtype=jnp.float32) * (-math.log(10000.0) / half))
    angles = jnp.arange(count, dtype=jnp.float32)[:, None] * frequency[None, :]
    cosine, sine = jnp.cos(angles), jnp.sin(angles)
    cosine = jnp.concatenate([cosine] * 4, axis=1)
    sine = jnp.concatenate([-sine, sine, -sine, sine], axis=1)
    shape = (count // TOK_DEV, TOK_DEV, PAIR)
    return (cosine.reshape(shape), sine.reshape(shape))


ROWS = 256
norm_epsilon = 1e-05


def row_loop(count, body, carry):
    size = min(ROWS, count)
    return lax.fori_loop(
        0, count // size, lambda i, c: body(pl.ds(pl.multiple_of(i * size, size), size), c), carry
    )


def normal(values):
    centred = values - jnp.mean(values, axis=-1, keepdims=True)
    inverse = lax.rsqrt(jnp.mean(centred * centred, axis=-1, keepdims=True) + norm_epsilon)
    return (centred * inverse, inverse)


def norm_back(values, grad, gain):
    shape, inverse = normal(values)
    inner = grad * gain
    result = inverse * (
        inner
        - jnp.mean(inner, axis=-1, keepdims=True)
        - shape * jnp.mean(inner * shape, axis=-1, keepdims=True)
    )
    return (
        result,
        jnp.sum(grad * shape, axis=0, keepdims=True),
        jnp.sum(grad, axis=0, keepdims=True),
    )


def fixed(shape):
    return pl.BlockSpec(shape, lambda i: (0,) * len(shape), pipeline_mode=pl.Buffered(1))


def output_spec(block, model):
    return pl.BlockSpec((model, model), lambda i: (0, block), pipeline_mode=pl.Buffered(1))


def project_in_kernel(x_ref, vec_ref, cos_ref, sin_ref, wq_ref, wk_ref, wv_ref, normed_ref, *outs):
    tokens = x_ref.shape[0]

    @pl.when(pl.program_id(0) == 0)
    def _():
        def body(rows, carry):
            shape, _ = normal(x_ref[rows, :].astype(jnp.float32))
            normed_ref[rows, :] = (shape * vec_ref[0:1, :] + vec_ref[4:5, :]).astype(jnp.bfloat16)
            return carry

        row_loop(tokens, body, 0)

    for at, weight_ref in enumerate((wq_ref, wk_ref, wv_ref)):
        made = mul(normed_ref[...], weight_ref[...], NN)
        for pair, out in enumerate(outs):
            part = made[:, pair * PAIR : (pair + 1) * PAIR]
            if at < 2:
                part = turn(part, cos_ref[...], sin_ref[...])
            out[0, :, at * PAIR : (at + 1) * PAIR] = part.astype(jnp.bfloat16)


def weight_spec(weight, first, model):
    return pl.BlockSpec((model, model // SPANS), lambda r: (0, first + r))


def project_in(x, vectors, cosine, sine, weights):
    tokens, model = x.shape
    piece = pl.BlockSpec((1, tokens, 3 * PAIR), lambda r: (r, 0, 0))
    result = pl.pallas_call(
        project_in_kernel,
        grid=(SPANS,),
        in_specs=[fixed(x.shape), fixed(vectors.shape), fixed(cosine.shape), fixed(sine.shape)]
        + [weight_spec(weight, first, model) for weight, first in weights],
        out_specs=[fixed((tokens, model))] + [piece] * PAIRS,
        out_shape=[jax.ShapeDtypeStruct((tokens, model), jnp.bfloat16)]
        + [jax.ShapeDtypeStruct((SPANS, tokens, 3 * PAIR), jnp.bfloat16)] * PAIRS,
        compiler_params=pltpu.CompilerParams(vmem_limit_bytes=VMEM),
        cost_estimate=lasts(10),
        name="project_in",
    )(x, vectors, cosine, sine, *[weight for weight, _ in weights])
    return (result[0], result[1:])


def project_back_kernel(*refs):
    pieces, refs = refs[:PAIRS], refs[PAIRS:]
    x_ref, vec_ref, gh_ref, wq_ref, wk_ref, wv_ref, gx_ref, sums_ref, joined_ref, total = refs
    step = pl.program_id(0)
    tokens, model = x_ref.shape
    width = wq_ref.shape[1]
    made = None
    for at, weight_ref in enumerate((wq_ref, wk_ref, wv_ref)):
        part = jnp.concatenate(
            [piece[0, :, at * PAIR : (at + 1) * PAIR] for piece in pieces], axis=1
        )
        first = at * model + step * width
        joined_ref[:, pl.ds(pl.multiple_of(first, width), width)] = part
        one = mul(part, weight_ref[...], NT)
        made = one if made is None else made + one

    @pl.when(step == 0)
    def _():
        total[...] = made

    @pl.when(step > 0)
    def _():
        total[...] += made

    @pl.when(step == SPANS - 1)
    def _():
        def body(rows, carry):
            back, gain, bias = norm_back(
                x_ref[rows, :].astype(jnp.float32), total[rows, :], vec_ref[0:1, :]
            )
            gx_ref[rows, :] = gh_ref[rows, :] + back
            return (carry[0] + gain, carry[1] + bias)

        zero = jnp.zeros((1, model), jnp.float32)
        gain, bias = row_loop(tokens, body, (zero, zero))
        sums_ref[...] = jnp.zeros_like(sums_ref)
        sums_ref[0:1, :] = gain
        sums_ref[4:5, :] = bias


def project_back(pieces, x, vectors, grad_middle, weights):
    tokens, model = x.shape
    return pl.pallas_call(
        project_back_kernel,
        grid=(SPANS,),
        in_specs=[pl.BlockSpec((1, tokens, 3 * PAIR), lambda r: (r, 0, 0))] * PAIRS
        + [fixed(x.shape), fixed(vectors.shape), fixed(x.shape)]
        + [weight_spec(weight, first, model) for weight, first in weights],
        out_specs=[fixed(x.shape), fixed((8, model)), fixed((tokens, 3 * model))],
        scratch_shapes=[pltpu.VMEM((tokens, model), jnp.float32)],
        out_shape=[
            jax.ShapeDtypeStruct((tokens, model), jnp.float32),
            jax.ShapeDtypeStruct((8, model), jnp.float32),
            jax.ShapeDtypeStruct((tokens, 3 * model), jnp.bfloat16),
        ],
        compiler_params=pltpu.CompilerParams(vmem_limit_bytes=VMEM),
        cost_estimate=lasts(13),
        name="project_back",
    )(*pieces, x, vectors, grad_middle, *[weight for weight, _ in weights])


def gelu_parts(z):
    root = math.sqrt(2.0 / math.pi)
    square = z * z
    bent = jnp.tanh(root * z * (1.0 + 0.044715 * square))
    half = 0.5 * (1.0 + bent)
    slope = half + 0.5 * z * (1.0 - bent * bent) * (root * (1.0 + 3.0 * 0.044715 * square))
    return (z * half, slope)


FF_TILE = 1024
FOLD = 32


def unfold(folded, flat=None):
    if flat is None:
        return folded
    count, columns = flat.shape
    times = folded.shape[1] // columns
    for slot in range(folded.shape[0] // FOLD):
        for at in range(times):
            flat[(slot * times + at) * FOLD : (slot * times + at + 1) * FOLD, :] = folded[
                slot * FOLD : (slot + 1) * FOLD, at * columns : (at + 1) * columns
            ]
    return flat


def down_specs(weight, model, hidden):
    array, block = weight
    if array.shape == (hidden, model):
        return (pl.BlockSpec((FF_TILE, model), lambda i: (i, 0)), [])
    rows = FF_TILE * model // hidden
    return (
        pl.BlockSpec((rows, hidden), lambda i: (i, block)),
        [pltpu.VMEM((FF_TILE, model), jnp.bfloat16)],
    )


def feed_kernel(*refs):
    pieces, refs = refs[:PAIRS], refs[PAIRS:]
    x_ref, vec_ref, wo_ref, up_ref, down_ref = refs[:5]
    joined_ref, u_ref, h_ref, c_ref, f_ref, slope_ref, m_ref, y_ref = refs[5:13]
    flat = refs[13:]
    down_ref = unfold(down_ref, *flat)
    step = pl.program_id(0)
    tokens = x_ref.shape[0]

    @pl.when(step == 0)
    def _():
        for pair in range(PAIRS):
            for at in range(SPANS):
                first = (at * PAIRS + pair) * PAIR
                joined_ref[:, first : first + PAIR] = pieces[pair][at]
        u_ref[...] = mul(joined_ref[...], wo_ref[...], NN)

        def body(rows, carry):
            shape, _ = normal(u_ref[rows, :])
            middle = x_ref[rows, :].astype(jnp.float32) + shape * vec_ref[1:2, :] + vec_ref[5:6, :]
            h_ref[rows, :] = middle
            shape, _ = normal(middle)
            c_ref[rows, :] = (shape * vec_ref[2:3, :] + vec_ref[6:7, :]).astype(jnp.bfloat16)
            return carry

        row_loop(tokens, body, 0)

    @pl.when(step == 0)
    def _():
        m_ref[...] = jnp.zeros_like(m_ref)

    made, slope = gelu_parts(mul(c_ref[...], up_ref[...], NN))
    slope_ref[...] = slope.astype(jnp.bfloat16)
    made = made.astype(jnp.bfloat16)
    f_ref[...] = made
    m_ref[...] += mul(made, down_ref[...], NN)

    @pl.when(step == pl.num_programs(0) - 1)
    def _():
        def body(rows, carry):
            shape, _ = normal(m_ref[rows, :])
            result = h_ref[rows, :] + shape * vec_ref[3:4, :] + vec_ref[7:8, :]
            y_ref[rows, :] = result.astype(jnp.bfloat16)
            return carry

        row_loop(tokens, body, 0)


def feed(pieces, x, vectors, output_weight, up_weight, down_weight):
    tokens, model = x.shape
    hidden = 4 * model
    full = lambda kind, columns=model: jax.ShapeDtypeStruct((tokens, columns), kind)
    wide = pl.BlockSpec((tokens, FF_TILE), lambda i: (0, i))
    down_spec, flat = down_specs(down_weight, model, hidden)
    return pl.pallas_call(
        feed_kernel,
        grid=(hidden // FF_TILE,),
        in_specs=[fixed((SPANS, tokens, PAIR))] * PAIRS
        + [fixed(x.shape), fixed(vectors.shape), output_spec(output_weight[1], model)]
        + [
            pl.BlockSpec((model, FF_TILE), lambda i: (0, i)),
            down_spec,
        ],
        out_specs=[fixed(x.shape)] * 4 + [wide, wide] + [fixed(x.shape)] * 2,
        scratch_shapes=flat,
        out_shape=[
            full(jnp.bfloat16),
            full(jnp.float32),
            full(jnp.float32),
            full(jnp.bfloat16),
            full(jnp.bfloat16, hidden),
            full(jnp.bfloat16, hidden),
            full(jnp.float32),
            full(jnp.bfloat16),
        ],
        compiler_params=pltpu.CompilerParams(vmem_limit_bytes=VMEM),
        cost_estimate=lasts(24),
        name="feed",
    )(*pieces, x, vectors, output_weight[0], up_weight, down_weight[0])


def feed_back_kernel(*refs):
    gy_ref, m_ref, h_ref, u_ref, vec_ref, wo_ref, slope_ref, down_ref, up_ref = refs[:9]
    gm_ref, gz_ref, gh_ref, gu_ref, sums_ref = refs[9:14]
    pieces = refs[14 : 14 + PAIRS]
    total, back, *flat = refs[14 + PAIRS :]
    down_ref = unfold(down_ref, *flat)
    step = pl.program_id(0)
    tokens, model = gy_ref.shape
    zero = jnp.zeros((1, model), jnp.float32)

    @pl.when(step == 0)
    def _():
        def body(rows, carry):
            grad, gain, bias = norm_back(m_ref[rows, :], gy_ref[rows, :], vec_ref[3:4, :])
            gm_ref[rows, :] = grad.astype(jnp.bfloat16)
            return (carry[0] + gain, carry[1] + bias)

        gain, bias = row_loop(tokens, body, (zero, zero))
        sums_ref[0:1, :] = zero
        sums_ref[4:5, :] = zero
        sums_ref[3:4, :] = gain
        sums_ref[7:8, :] = bias

    @pl.when(step == 0)
    def _():
        total[...] = jnp.zeros_like(total)

    made = mul(gm_ref[...], down_ref[...], NT) * slope_ref[...].astype(jnp.float32)
    made = made.astype(jnp.bfloat16)
    gz_ref[...] = made
    total[...] += mul(made, up_ref[...], NT)

    @pl.when(step == pl.num_programs(0) - 1)
    def _():
        def body(rows, carry):
            grad, gain_two, bias_two = norm_back(h_ref[rows, :], total[rows, :], vec_ref[2:3, :])
            middle = gy_ref[rows, :] + grad
            gh_ref[rows, :] = middle
            grad, gain_one, bias_one = norm_back(u_ref[rows, :], middle, vec_ref[1:2, :])
            gu_ref[rows, :] = grad.astype(jnp.bfloat16)
            new = (gain_one, gain_two, bias_one, bias_two)
            return tuple(old + more for old, more in zip(carry, new))

        gain_one, gain_two, bias_one, bias_two = row_loop(tokens, body, (zero,) * 4)
        sums_ref[1:2, :] = gain_one
        sums_ref[2:3, :] = gain_two
        sums_ref[5:6, :] = bias_one
        sums_ref[6:7, :] = bias_two
        back[...] = mul(gu_ref[...], wo_ref[...], NT).astype(jnp.bfloat16)
        for pair in range(PAIRS):
            for at in range(SPANS):
                first = (at * PAIRS + pair) * PAIR
                pieces[pair][at] = back[:, first : first + PAIR]


def feed_back(grad, m, h, u, vectors, output_weight, slope, down_weight, up_weight):
    tokens, model = grad.shape
    hidden = 4 * model
    full = lambda kind, columns=model: jax.ShapeDtypeStruct((tokens, columns), kind)
    wide = pl.BlockSpec((tokens, FF_TILE), lambda i: (0, i))
    down_spec, flat = down_specs(down_weight, model, hidden)
    result = pl.pallas_call(
        feed_back_kernel,
        grid=(hidden // FF_TILE,),
        in_specs=[fixed(grad.shape)] * 4
        + [fixed(vectors.shape), output_spec(output_weight[1], model), wide]
        + [
            down_spec,
            pl.BlockSpec((model, FF_TILE), lambda i: (0, i)),
        ],
        out_specs=[fixed(grad.shape), wide, fixed(grad.shape), fixed(grad.shape)]
        + [fixed((8, model))]
        + [fixed((SPANS, tokens, PAIR))] * PAIRS,
        scratch_shapes=[
            pltpu.VMEM((tokens, model), jnp.float32),
            pltpu.VMEM((tokens, model), jnp.bfloat16),
            *flat,
        ],
        out_shape=[
            full(jnp.bfloat16),
            full(jnp.bfloat16, hidden),
            full(jnp.float32),
            full(jnp.bfloat16),
            jax.ShapeDtypeStruct((8, model), jnp.float32),
        ]
        + [jax.ShapeDtypeStruct((SPANS, tokens, PAIR), jnp.bfloat16)] * PAIRS,
        compiler_params=pltpu.CompilerParams(vmem_limit_bytes=VMEM),
        cost_estimate=lasts(26),
        name="feed_back",
    )(grad, m, h, u, vectors, output_weight[0], slope, down_weight[0], up_weight)
    return (result[:5], list(result[5:]))


def weave_kernel(mine, own_ref, other_ref, out_ref):
    count = own_ref.shape[1]
    first = pl.multiple_of(mine[0] * count, count)
    second = pl.multiple_of((1 - mine[0]) * count, count)
    out_ref[0, pl.ds(first, count), :] = own_ref[0]
    out_ref[0, pl.ds(second, count), :] = other_ref[0]


def weave(own, other, mine):
    outer, count, columns = own.shape
    if count % 16 or columns % 128:
        return jnp.where(
            mine == 0, jnp.concatenate([own, other], axis=1), jnp.concatenate([other, own], axis=1)
        )
    spec = pl.BlockSpec((1, count, columns), lambda i, s: (i, 0, 0))
    return pl.pallas_call(
        weave_kernel,
        grid_spec=pltpu.PrefetchScalarGridSpec(
            num_scalar_prefetch=1,
            grid=(outer,),
            in_specs=[spec, spec],
            out_specs=pl.BlockSpec((1, 2 * count, columns), lambda i, s: (i, 0, 0)),
        ),
        out_shape=jax.ShapeDtypeStruct((outer, 2 * count, columns), own.dtype),
        compiler_params=pltpu.CompilerParams(vmem_limit_bytes=VMEM),
        cost_estimate=lasts(3),
        name="weave",
    )(jnp.reshape(mine, (1,)), own, other)


def half_kernel(which, *refs, far, near, start):
    lefts, (right_ref, *more, out_ref, turned) = refs[:far], refs[far:]

    @pl.when(pl.program_id(0) == 0)
    def _():
        for at, left_ref in enumerate(lefts):
            size = left_ref.shape[1]
            turned[at * size : (at + 1) * size, :] = jnp.transpose(left_ref[...])

    made = mul(turned[...], right_ref[...], NN)
    if not more:
        out_ref[...] = made.astype(out_ref.dtype)
        return
    made = (made + more[0][...].astype(jnp.float32)).astype(out_ref.dtype)
    rows = out_ref.shape[2]
    for z in range(far):
        for f in range(near):
            at = (z * near + f) * rows
            out_ref[f, z] = made[at : at + rows]


def half_rows_kernel(which, left_ref, right_ref, *refs, near):
    out_ref = refs[-1]
    made = mul(left_ref[...], right_ref[...], TN)
    if len(refs) == 1:
        out_ref[...] = made.astype(out_ref.dtype)
        return
    made = (made + refs[0][...].astype(jnp.float32)).astype(out_ref.dtype)
    rows, columns = out_ref.shape[2], made.shape[1]
    for f in range(near):
        for q in range(out_ref.shape[3] // columns):
            at = f * (made.shape[0] // near) + q * rows
            out_ref[f, 0, :, q * columns : (q + 1) * columns] = made[at : at + rows]


def half_product(left, right, which, far, near, got=None, joint=None, start=0, width=0, rows=0):
    tokens, count = left.shape
    columns = right.shape[1]
    size = count // (2 * far)
    which = jnp.reshape(which, (1,))
    tall = size // near > rows if got is not None else count > columns
    tile = columns if tall else min(columns, 1024)
    if tall:
        grid = (far,)
        ins = [
            pl.BlockSpec((tokens, size), lambda i, w: (0, 2 * i + w[0])),
            pl.BlockSpec((tokens, columns), lambda i, w: (0, 0)),
        ]
        lefts, scratch = [left], []
        flat = pl.BlockSpec((size, columns), lambda i, w: (i, 0))
        wide = columns * (size // near // rows) if got is not None else 0
        spread = pl.BlockSpec((near, 1, rows, wide), lambda i, w: (0, i, 0, start // wide))
        kernel = functools.partial(half_rows_kernel, near=near)
    else:
        grid = (columns // tile,)
        ins = [
            pl.BlockSpec((tokens, size), lambda c, w, at=at: (0, 2 * at + w[0])) for at in range(far)
        ] + [pl.BlockSpec((tokens, tile), lambda c, w: (0, c))]
        lefts, scratch = [left] * far, [pltpu.VMEM((count // 2, tokens), jnp.bfloat16)]
        flat = pl.BlockSpec((count // 2, tile), lambda c, w: (0, c))
        spread = pl.BlockSpec((near, far, rows, tile), lambda c, w: (0, 0, 0, start // tile + c))
        kernel = functools.partial(half_kernel, far=far, near=near, start=start)
    operands, aliases = ([*lefts, right], {})
    if got is None:
        shape, out = (count // 2, columns), flat
    else:
        shape, out = (near, far, rows, width), spread
        operands.append(got)
        ins.append(flat)
        if joint is not None:
            plain = kernel
            kernel = lambda *refs: plain(*refs[: 1 + len(operands) - 1], *refs[1 + len(operands) :])
            operands.append(joint)
            ins.append(pl.BlockSpec(memory_space=pl.ANY))
            aliases = {len(operands): 0}
    return pl.pallas_call(
        kernel,
        grid_spec=pltpu.PrefetchScalarGridSpec(
            num_scalar_prefetch=1, grid=grid, in_specs=ins, out_specs=out, scratch_shapes=scratch
        ),
        out_shape=jax.ShapeDtypeStruct(shape, jnp.bfloat16),
        input_output_aliases=aliases,
        compiler_params=pltpu.CompilerParams(vmem_limit_bytes=VMEM),
        cost_estimate=lasts(6),
        name="half_product",
    )(which, *operands)


def sizes():
    return (lax.axis_size("far"), lax.axis_size("core"), lax.axis_size("fsdp"))


def flip(array, axis, apart):
    return lax.ppermute(array, axis, [(i, i ^ apart) for i in range(lax.axis_size(axis))])


def swap_cores(array):
    return flip(array, "core", 1)


def after(values, *others):
    return lax.optimization_barrier((values, others))[0]


def exchange(pieces):
    count = lax.axis_size("fsdp")
    rows = [list(range(at, at + SPANS)) for at in range(0, count, SPANS)]
    return lax.all_to_all(
        pieces, "fsdp", 0, 0, axis_index_groups=rows if len(rows) > 1 else None, tiled=True
    )


class Gather:
    def __init__(self, part, inner_first):
        far, _, near = sizes()
        steps = lambda axis, count: [(axis, i) for i in range(count.bit_length() - 1)]
        inner = steps("fsdp", near)
        if inner_first:
            inner = inner[1::-1] + inner[2:]
        self.part = part
        self.order = steps("far", far)[::-1] + inner + [("core", 0)]
        self.place = {bit: at for at, bit in enumerate(steps("fsdp", near) + [("core", 0)] + steps("far", far))}
        self.held = []

    def send(self):
        bit = self.order.pop(0)
        outer = 2 ** sum(1 for other in self.held if self.place[other] > self.place[bit])
        rows, columns = self.part.shape
        self.own = self.part.reshape(outer, rows // outer, columns)
        self.other = flip(self.own, bit[0], 1 << bit[1])
        self.mine = lax.axis_index(bit[0]) >> bit[1] & 1
        self.held.append(bit)

    def take(self, *others):
        own = after(self.own, *others) if others else self.own
        outer, rows, columns = own.shape
        self.part = weave(own, self.other, self.mine).reshape(2 * outer * rows, columns)

    def run(self, count=None):
        for _ in range(len(self.order) if count is None else count):
            self.send()
            self.take()
        return self.part


class Reduction:
    def __init__(self, products, vectors=None):
        self.products, self.vectors = products, vectors
        far, core, near = sizes()
        self.rows = products[0][0].shape[1] // (far * core * near)
        self.plain = self.rows % 16 != 0
        self.stage = 0
        self.value, self.apart = ((), 0)
        if not self.plain:
            self.value = [
                half_product(left, right, 1 - lax.axis_index("core"), far, near)
                for left, right in products
            ]
            if vectors is not None:
                turned = jnp.pad(vectors.T, ((0, 0), (0, 128 - vectors.shape[0])))
                halves = turned.reshape(far, core, near, self.rows, 128)
                pick = lambda at: lax.dynamic_index_in_dim(halves, at, 1, keepdims=False)
                mine = lax.axis_index("core")
                self.value.append(pick(1 - mine))
                self.vectors = pick(mine)

    def swap(self):
        if not self.plain:
            self.got = [swap_cores(value) for value in self.value]
            self.value = ()

    def join(self):
        if self.plain:
            return
        far, core, near = sizes()
        block = self.rows * far * near
        extra = None
        if self.vectors is not None:
            extra = (self.vectors + self.got.pop()).astype(jnp.bfloat16).transpose(1, 0, 2, 3)
        width = sum(value.size for value in self.got) // block
        width += 0 if extra is None else 128
        joint, start = None, 0
        for (left, right), got in zip(self.products, self.got):
            joint = half_product(
                left, right, lax.axis_index("core"), far, near, got, joint, start, width, self.rows
            )
            start += got.size // block
        if extra is not None:
            joint = lax.dynamic_update_slice_in_dim(joint, extra, start, axis=3)
        self.value = joint

    def near(self, offload):
        if self.plain:
            return
        count, far, rows, width = self.value.shape
        flat = self.value.reshape(count * far * rows, width)
        if offload:
            self.value = lax.psum_scatter(flat, "fsdp", scatter_dimension=0, tiled=True)
        else:
            self.got = lax.all_to_all(flat, "fsdp", 0, 0, tiled=True).reshape(count, far * rows, width)

    def sent(self):
        return () if self.plain else (self.got,)

    def near_take(self, *others):
        if self.plain:
            return
        got = after(self.got, *others) if others else self.got
        self.value = jnp.sum(got.astype(jnp.float32), axis=0).astype(jnp.bfloat16)

    def send(self):
        if self.plain:
            return
        if self.apart == 0:
            self.value = self.value.reshape(-1, self.rows, self.value.shape[-1])
            self.apart = 1
        mine = lax.axis_index("far") // self.apart % 2
        split = self.value.reshape(self.value.shape[0] // 2, 2, *self.value.shape[1:])
        pick = lambda at: lax.dynamic_index_in_dim(split, at, 1, keepdims=False)
        self.got = flip(pick(1 - mine), "far", self.apart)
        self.value = pick(mine)
        self.apart *= 2

    def take(self, *others):
        if self.plain:
            return
        kept = after(self.value, *others) if others else self.value
        value = kept.astype(jnp.float32) + self.got.astype(jnp.float32)
        self.value = value.astype(jnp.bfloat16) if value.shape[0] > 1 else value

    def rest(self):
        while not self.plain and self.value.shape[0] > 1:
            self.send()
            self.take()

    def result(self):
        if self.plain:
            sums = [
                lax.psum_scatter(
                    product_rows(left, right), ("far", "core", "fsdp"), scatter_dimension=0, tiled=True
                )
                for left, right in self.products
            ]
            if self.vectors is not None:
                axes = ("far", "core", "fsdp")
                sums.append(lax.psum_scatter(self.vectors, axes, scatter_dimension=1, tiled=True))
            return sums
        total = jnp.sum(self.value.astype(jnp.float32), axis=0)
        sums, first = ([], 0)
        for left, right in self.products:
            count = left.shape[1] // self.products[0][0].shape[1]
            columns = right.shape[1]
            part = total[:, first : first + count * columns]
            part = part.reshape(self.rows, count, columns).transpose(1, 0, 2)
            sums.append(part.reshape(count * self.rows, columns))
            first += count * columns
        if self.vectors is not None:
            sums.append(total[:, first:])
        return sums


def tie(main, *reductions):
    main, values = lax.optimization_barrier((main, [reduction.value for reduction in reductions]))
    for reduction, value in zip(reductions, values):
        reduction.value = value
    return main


def body(
    hidden_in,
    w_query,
    w_key,
    w_value,
    w_output,
    w_up,
    w_down,
    norm_gain,
    norm_bias,
    grad_out,
    group_id,
    group_scale,
    span_place,
):
    far, core, near = sizes()
    slot_index = (lax.axis_index("far") * core + lax.axis_index("core")) * near + lax.axis_index("fsdp")
    sources = slot_index // SPANS * SPANS + jnp.arange(SPANS, dtype=jnp.int32)
    slot_ids = jnp.arange(span_place.shape[0], dtype=jnp.int32)
    places = jnp.sum(jnp.where(sources[:, None] == slot_ids[None, :], span_place[None, :], 0), axis=1)
    own_place = jnp.sum(jnp.where(slot_ids == slot_index, span_place, 0))
    tables = turning_tables(SPANS * TOK_DEV)
    cosine, sine = [lax.dynamic_index_in_dim(t, own_place, 0, keepdims=False) for t in tables]

    side = lambda parts: jnp.concatenate(parts, axis=1)
    whole = lambda part: lax.all_gather(part, ("far", "core", "fsdp"), axis=0, tiled=True)
    small = jnp.concatenate([norm_gain, norm_bias], axis=1)
    vector_count = small.shape[0] * small.shape[1]
    small = small.reshape(vector_count, small.shape[2]).T
    small = jnp.pad(small, ((0, 0), (0, 128 - vector_count)))
    query_key = Gather(side([w_query[1], w_key[1]]), False)
    value_output = Gather(side([w_value[1], w_output[1]]), True)
    late = (query_key, value_output)
    begun = [gather.run(3) for gather in late]
    folds = w_up.shape[1] % FOLD == 0

    def gather_outer(layer):
        up_part, down_part = w_up[layer], w_down[layer]
        if not folds:
            return (whole(up_part), (whole(down_part), 0))
        rows, columns = up_part.shape
        folded = down_part.reshape(columns // down_part.shape[1], rows, down_part.shape[1])
        folded = folded.transpose(1, 0, 2).reshape(rows, columns)
        joint = whole(side([up_part, folded]))
        return (joint, (joint, 1))

    first = whole(side([w_query[0], w_key[0], w_value[0], w_output[0], small]))
    outer_first_weights, outer_second_weights = (gather_outer(0), gather_outer(1))
    vectors = first[:, 4 * w_query.shape[2] :][:, :vector_count].T.astype(jnp.float32)
    vectors = vectors.reshape(2, 8, vectors.shape[1])

    def forward_layer(layer, hidden, joined, begin, middle, rest):
        normed, sent = project_in(hidden, vectors[layer], cosine, sine, joined)
        sent = begin(list(sent))
        pieces = [exchange(sent[0])]
        pieces.append(exchange(sent[1]))
        attended, totals, back = ([], [], [])
        for pair in range(PAIRS):
            outs, total = attend(places, pieces[pair])
            if pair == 0:
                outs, pieces[1] = lax.optimization_barrier((outs, pieces[1]))
            attended.append(outs)
            totals.append(total)
            back.append(exchange(outs))
        middle(outs)
        joined_heads, u, h, c, f, slope, m, y = feed(back, hidden, vectors[layer], *rest)
        kept = (hidden, normed, pieces, attended, totals, joined_heads, u, h, c, f, slope, m, joined, rest)
        return (y, kept)

    def begin_late(sent):
        sent, begun_parts = lax.optimization_barrier((sent, begun))
        for gather, part in zip(late, begun_parts):
            gather.part = part
            gather.send()
        return sent

    def take_late(outs):
        for gather in late:
            gather.take(outs)
            gather.send()

    hidden_mid, kept_first = forward_layer(
        0,
        hidden_in,
        [(first, 0), (first, SPANS), (first, 2 * SPANS)],
        begin_late,
        take_late,
        ((first, 3), *outer_first_weights),
    )
    for gather in late:
        gather.take(hidden_mid)
        gather.run()
    hidden_out, kept_second = forward_layer(
        1,
        hidden_mid,
        [(query_key.part, 0), (query_key.part, SPANS), (value_output.part, 0)],
        lambda sent: sent,
        lambda outs: None,
        ((value_output.part, 1), *outer_second_weights),
    )

    row_index = slot_index // SPANS
    row_ids = jnp.arange(group_id.shape[0], dtype=jnp.int32)
    group_of_row = jnp.sum(jnp.where(row_ids == row_index, group_id, 0))
    group_ids = jnp.arange(group_scale.shape[0], dtype=jnp.int32)
    row_scale = jnp.sum(jnp.where(group_ids == group_of_row, group_scale, 0.0))
    grad = grad_out.astype(jnp.float32) * row_scale

    def backward_layer(layer, grad, kept, points, vector_terms=None):
        hidden, normed, pieces, attended, totals, joined_heads, u, h, c, f, slope, m, joined, weights = kept
        output_weight, up_weight, down_weight = weights
        made, there = feed_back(
            grad, m, h, u, vectors[layer], output_weight, slope, down_weight, up_weight
        )
        gm, gz, grad_middle, gu, sums = made
        outer = Reduction([(c, gz), (f, gm), (joined_heads, gu)])
        there[0] = exchange(there[0])
        there = points[0](there, outer)
        there = list(there)
        if layer:
            there[1] = exchange(there[1])
        outer.swap()
        outs = attend_back(places, pieces[0], there[0], attended[0], *tables, totals[0])
        outer.join()
        if layer == 0:
            there[1] = exchange(after(there[1], outs, outer.value, *inner_second.sent()))
        outs, there = points[1]((outs, there), outer)
        if layer == 0:
            outer.near(True)
        grads = [exchange(outs)]
        outs = attend_back(places, pieces[1], there[1], attended[1], *tables, totals[1])
        outs, grads = lax.optimization_barrier((outs, grads))
        points[2](outs)
        grads.append(exchange(outs))
        grads = points[4](grads, outer)
        if layer:
            outer.near(True)
        grad_in, more, joined_grad = project_back(
            grads, hidden, vectors[layer], grad_middle, joined
        )
        sums = sums + more
        if vector_terms is not None:
            vector_terms = jnp.concatenate([sums, vector_terms], axis=0)
        inner = Reduction([(normed, joined_grad)], vector_terms)
        grad_in = points[3](grad_in, inner)
        inner.swap()
        inner.join()
        return (grad_in, sums, outer, inner)

    grad, sums_second, outer_second, inner_second = backward_layer(
        1, grad, kept_second, [tie, tie, lambda outs: None, tie, tie]
    )
    grad = tie(grad, inner_second)

    def after_feed(main, outer):
        main = tie(main, inner_second, outer)
        inner_second.near(False)
        return main


    def after_pair(main, outer):
        inner_second.near_take(main)
        main = tie(main, outer, outer_second, inner_second)
        outer_second.send()
        inner_second.send()
        return main

    def after_pairs(outs):
        outer_second.take(outs)
        outer_second.send()
        inner_second.take(outs)
        inner_second.send()

    def after_return(grads, outer):
        outer_second.take()
        inner_second.take()
        return tie(grads, outer_second, inner_second)

    grad_in, _, outer_first, inner_first = backward_layer(
        0, grad, kept_first, [after_feed, after_pair, after_pairs, tie, after_return], sums_second
    )
    outer_first.value = after(outer_first.value, inner_first.value)
    inner_first.near(False)
    outer_first.send()
    outer_first.take()
    inner_first.near_take(outer_first.value)
    outer_first.rest()
    inner_first.rest()
    up_pair, down_pair, output_pair = zip(outer_first.result(), outer_second.result())
    joined_first, vector_terms = inner_first.result()
    if not inner_first.plain:
        vector_terms = vector_terms[:, :16].T
    vector_terms = vector_terms.reshape(2, 2, 4, vector_terms.shape[1])
    joined_pair = jnp.stack([joined_first, inner_second.result()[0]])
    width = hidden_in.shape[1]
    return (
        hidden_mid,
        hidden_out,
        grad_in,
        joined_pair[:, :, :width],
        joined_pair[:, :, width : 2 * width],
        joined_pair[:, :, 2 * width :],
        jnp.stack(output_pair),
        jnp.stack(up_pair),
        jnp.stack(down_pair),
        vector_terms[:, 0],
        vector_terms[:, 1],
    )


def solution(mesh):
    count, near = mesh.devices.shape
    mesh = Mesh(mesh.devices.reshape(count // 2, 2, near), ("far", "core", "fsdp"))
    placed = (
        P(("far", "core", "fsdp"), None),
        P(None, ("far", "core", "fsdp"), None),
        P(None, ("far", "core", "fsdp"), None),
        P(None, ("far", "core", "fsdp"), None),
        P(None, ("far", "core", "fsdp"), None),
        P(None, ("far", "core", "fsdp"), None),
        P(None, ("far", "core", "fsdp"), None),
        P(None, None, ("far", "core", "fsdp")),
        P(None, None, ("far", "core", "fsdp")),
        P(("far", "core", "fsdp"), None),
        P(),
        P(),
        P(),
    )
    return jax.shard_map(
        body,
        mesh=mesh,
        in_specs=placed,
        out_specs=(
            P(("far", "core", "fsdp"), None),
            P(("far", "core", "fsdp"), None),
            P(("far", "core", "fsdp"), None),
            P(None, ("far", "core", "fsdp"), None),
            P(None, ("far", "core", "fsdp"), None),
            P(None, ("far", "core", "fsdp"), None),
            P(None, ("far", "core", "fsdp"), None),
            P(None, ("far", "core", "fsdp"), None),
            P(None, ("far", "core", "fsdp"), None),
            P(None, None, ("far", "core", "fsdp")),
            P(None, None, ("far", "core", "fsdp")),
        ),
        check_vma=False,
    )
```
